256 devices in a mesh: ctx: 16 (over z, x_hi), tp: 16 (over y, x_lo, core).
Axes of the slice: x: 4 (x_hi: 2, x_lo: 2; x = x_hi * 2 + x_lo), y: 4, z: 8, core: 2. Of those that a mesh axis runs over, the one named last changes fastest.
Arguments:
- grad_out: bfloat16 [4096, 4096], P('tp', 'ctx'), may hold values from -6 to 6
- out_weight: bfloat16 [4096, 4096], P('tp'), may hold values from -0.09375 to 0.09375
- gate: bfloat16 [4096, 4096], P('tp', 'ctx'), may hold values from -6 to 6
- key_in: bfloat16 [4096, 4096], P('tp', 'ctx'), may hold values from -0.59765625 to 0.59765625
- value_in: bfloat16 [4096, 4096], P('tp', 'ctx'), may hold values from -0.59765625 to 0.59765625
- conv_out: bfloat16 [4096, 4096], P('tp', 'ctx'), may hold values from -0.75 to 0.75
- filt: bfloat16 [4096, 4096], P('tp', 'ctx'), may hold values from -0.09375 to 0.09375
- skip_bias: float32 [4096], P('tp'), may hold values from -4 to 4
Outputs:
- gate_grad: bfloat16 [4096, 4096], P('tp', 'ctx')
- key_grad: bfloat16 [4096, 4096], P('tp', 'ctx')
- value_grad: bfloat16 [4096, 4096], P('tp', 'ctx')
- filter_grad: bfloat16 [4096, 4096], P('tp', 'ctx')
- weight_grad: float32 [4096, 4096], P('tp', 'ctx')
- bias_grad: float32 [4096], P('tp')
The draws below stay inside these ranges and needn't reach their ends.
All inputs are finite; a program needn't handle non-finite values.
Results may differ from the reference program's by a relative error of at most 0.015.
Values may be sent and summed in bfloat16 or wider, within the bound.
No kernel may reach another device: no remote copies, remote signals or barrier semaphores. Data moves between devices by JAX's collectives and lax.ppermute only.
A program may use at most 64 MiB of HBM per device.

```python
import jax
import jax.numpy as jnp
from jax import lax

D = 4096
SEQ = 4096


def block_scale(own_key, shape, cuts, smallest, high):
    def one(axis_at, parts):
        draws = jax.random.uniform(jax.random.fold_in(jax.random.fold_in(own_key, 6), axis_at), (parts,), jnp.float32, smallest / len(cuts), high / len(cuts))
        return jnp.repeat(jnp.exp(draws), shape[axis_at] // parts).reshape((-1,) + (1,) * (len(shape) - axis_at - 1))

    level = one(*cuts[0])
    for cut in cuts[1:]:
        level = level * one(*cut)
    return level


def centred(own_key, extent, scale, reach, split=(), kind=jnp.bfloat16):
    values = scale * jax.random.normal(own_key, extent, jnp.float32)
    if split:
        values = values * block_scale(own_key, extent, split, -0.22, 0.18)
    return jnp.clip(values, -reach, reach).astype(kind)


def setup_inputs(seed: int = 0) -> dict:
    arg_keys = jax.random.split(jax.random.key(seed), 9)
    return {
        "grad_out": centred(arg_keys[0], (D, SEQ), 1.0, 6.0, ((0, 16), (1, 16))),
        "out_weight": centred(arg_keys[1], (D, D), D ** -0.5, 0.09375, ((0, 16),)),
        "gate": centred(arg_keys[2], (D, SEQ), 1.0, 6.0, ((0, 16), (1, 16))),
        "key_in": centred(arg_keys[3], (D, SEQ), 0.1, 0.59765625, ((0, 16), (1, 16))),
        "value_in": centred(arg_keys[4], (D, SEQ), 0.1, 0.59765625, ((0, 16), (1, 16))),
        "conv_out": centred(arg_keys[5], (D, SEQ), 0.125, 0.75, ((0, 16), (1, 16))),
        "filt": centred(arg_keys[6], (D, SEQ), SEQ ** -0.5, 0.09375, ((0, 16), (1, 16))),
        "skip_bias": centred(arg_keys[7], (D,), 1.0, 4.0, ((0, 16),), jnp.float32),
    }


def conv_block(pieces):
    grad_blk, prod_blk, filt_blk = pieces
    seq_len = grad_blk.shape[1]
    fft_len = 2 * seq_len
    spec_grad = jnp.fft.rfft(grad_blk, n=fft_len, axis=1)
    spec_prod = jnp.fft.rfft(prod_blk, n=fft_len, axis=1)
    spec_filt = jnp.fft.rfft(filt_blk, n=fft_len, axis=1)
    filt_part = jnp.fft.irfft(spec_grad * jnp.conj(spec_prod), n=fft_len, axis=1)[:, :seq_len]
    conv_part = jnp.fft.irfft(spec_grad * jnp.conj(spec_filt), n=fft_len, axis=1)[:, :seq_len]
    bias_part = jnp.sum(grad_blk * prod_blk, axis=1)
    return filt_part.astype(grad_blk.dtype), conv_part.astype(grad_blk.dtype), bias_part


def reference(grad_out, out_weight, gate, key_in, value_in, conv_out, filt, skip_bias):
    grad_gated = jnp.dot(out_weight, grad_out, preferred_element_type=jnp.float32)
    gate_grad = (grad_gated * conv_out.astype(jnp.float32)).astype(jnp.bfloat16)
    conv_out_grad = lax.optimization_barrier((grad_gated * gate.astype(jnp.float32)).astype(jnp.bfloat16))
    gated = (gate.astype(jnp.float32) * conv_out.astype(jnp.float32)).astype(jnp.bfloat16)
    weight_grad = jnp.dot(gated, grad_out.T, preferred_element_type=jnp.float32)
    product = lax.optimization_barrier((key_in.astype(jnp.float32) * value_in.astype(jnp.float32)).astype(jnp.bfloat16))
    block_rows = 128
    grad_wide = conv_out_grad.astype(jnp.float32).reshape(D // block_rows, block_rows, SEQ)
    prod_wide = product.astype(jnp.float32).reshape(D // block_rows, block_rows, SEQ)
    filt_wide = filt.astype(jnp.float32).reshape(D // block_rows, block_rows, SEQ)
    filt_all, conv_all, bias_all = lax.map(conv_block, (grad_wide, prod_wide, filt_wide))
    filter_grad = filt_all.reshape(D, SEQ).astype(jnp.bfloat16)
    conv_back = lax.optimization_barrier(conv_all.reshape(D, SEQ).astype(jnp.bfloat16))
    product_grad = (conv_back.astype(jnp.float32) + skip_bias[:, None].astype(jnp.float32) * conv_out_grad.astype(jnp.float32)).astype(jnp.bfloat16)
    key_grad = (product_grad.astype(jnp.float32) * value_in.astype(jnp.float32)).astype(jnp.bfloat16)
    value_grad = (product_grad.astype(jnp.float32) * key_in.astype(jnp.float32)).astype(jnp.bfloat16)
    bias_grad = bias_all.reshape(D).astype(jnp.float32)
    return (gate_grad, key_grad, value_grad, filter_grad, weight_grad, bias_grad)
```

```python
import functools
import math

import jax
import jax.numpy as jnp
import numpy as np
from jax import lax
from jax.experimental import pallas as pl
from jax.experimental.pallas import tpu as pltpu
from jax.sharding import PartitionSpec as P

bf16 = jnp.bfloat16
f32 = jnp.float32


def hi_lo(table):
    high = table.astype(np.float32).astype(bf16)
    low = (table - high.astype(np.float64)).astype(np.float32).astype(bf16)
    return high, low


def dft_tables(blocks, width):
    full = 2 * blocks
    k = np.arange(full)[:, None]
    a = np.arange(blocks)[None, :]
    b = np.arange(width)
    outer = np.exp(-2j * np.pi * ((k * a) % full) / full)
    twist = np.exp(-2j * np.pi * ((k * b[None, :]) % (full * width)) / (full * width))
    inner = np.exp(-2j * np.pi * ((b[:, None] * b[None, :]) % width) / width)
    return outer, twist, inner


def spectral_kernel(g_ref, p_ref, f_ref, a_ref, at_ref, b_ref, tw_ref, out_ref, *, per, blocks, width):
    rows = 2 * blocks * per
    half = blocks * per

    def dot(left, right):
        return jnp.dot(left, right, preferred_element_type=f32)

    def split(x):
        high = x.astype(bf16)
        return high, (x - high.astype(f32)).astype(bf16)

    def outer(x):
        return dot(a_ref[0], x) + dot(a_ref[1], x)

    g = g_ref[...].reshape(half, width)
    p = p_ref[...].reshape(half, width)
    f = f_ref[...].reshape(half, width)
    g1 = outer(g)
    p1 = outer(p)
    f1 = outer(f)
    tre = jnp.broadcast_to(tw_ref[0][:, None, :], (2 * blocks, per, width)).reshape(rows, width)
    tim = jnp.broadcast_to(tw_ref[1][:, None, :], (2 * blocks, per, width)).reshape(rows, width)

    def inner(re, im):
        rh, rl = split(re)
        ih, il = split(im)
        bh = b_ref[0]
        bl = b_ref[1]
        r = dot(rh, bh) + (dot(rl, bh) + dot(rh, bl))
        i = dot(ih, bh) + (dot(il, bh) + dot(ih, bl))
        return r[:, :width], r[:, width:], i[:, :width], i[:, width:]

    def forward(re, im):
        ur = re * tre - im * tim
        ui = re * tim + im * tre
        rr, ri, ir, ii = inner(ur, ui)
        return rr - ii, ri + ir

    gre, gim = forward(g1[:rows], g1[rows:])
    zre, zim = forward(p1[:rows] + f1[rows:], p1[rows:] - f1[:rows])
    ore = gre * zre + gim * zim
    oim = gim * zre - gre * zim
    rr, ri, ir, ii = inner(ore, oim)
    mre = rr + ii
    mim = ir - ri
    scale = 1.0 / (2 * blocks * width)
    bre = (mre * tre + mim * tim) * scale
    bim = (mim * tre - mre * tim) * scale
    rh, rl = split(bre)
    ih, il = split(bim)

    def back(x, which):
        ah = at_ref[0, which]
        al = at_ref[1, which]
        return dot(ah, x[0]) + (dot(al, x[0]) + dot(ah, x[1]))

    lag = back((rh, rl), 0) + back((ih, il), 1)
    conv = back((ih, il), 0) - back((rh, rl), 1)
    out_ref[:, :per, :] = lag.astype(bf16).reshape(blocks, per, width)
    out_ref[:, per : 2 * per, :] = conv.astype(bf16).reshape(blocks, per, width)
    prod = g.astype(f32) * p.astype(f32)
    total = jnp.sum(jnp.sum(prod.reshape(blocks, per, width), axis=0), axis=1, keepdims=True)
    high = total.astype(bf16).astype(f32)
    low = total - high
    eighth = per // 2
    lane = lax.broadcasted_iota(jnp.int32, (eighth, width), 1) // (width // 4)
    top = jnp.where(lane == 0, high[:eighth], jnp.where(lane == 1, low[:eighth], 0.0))
    low_part = jnp.where(lane == 2, high[eighth:], jnp.where(lane == 3, low[eighth:], 0.0))
    extra = (top + low_part).astype(bf16)
    out_ref[:, 2 * per :, :] = jnp.broadcast_to(extra[None], (blocks, eighth, width))


def spectral(g, p, f):
    blocks, per, width = g.shape
    rows = 2 * blocks * per
    outer, twist, inner = dft_tables(blocks, width)
    a_tab = np.stack([np.stack(hi_lo(part)) for part in (outer.real, outer.imag)], 1)
    a_tab = lax.optimization_barrier(jnp.asarray(a_tab))
    eye = jnp.eye(per, dtype=bf16)
    a_mat = (a_tab[:, :, :, None, :, None] * eye[:, None, :]).reshape(2, 2 * rows, blocks * per)
    at_tab = a_tab.transpose(0, 1, 3, 2)
    at_mat = (at_tab[:, :, :, None, :, None] * eye[:, None, :]).reshape(2, 2, blocks * per, rows)
    b_mat = jnp.asarray(np.stack(hi_lo(np.concatenate([inner.real, inner.imag], 1))))
    tw = jnp.asarray(np.stack([twist.real, twist.imag]).astype(np.float32))
    vm = pl.BlockSpec(memory_space=pltpu.VMEM)
    return pl.pallas_call(
        functools.partial(spectral_kernel, per=per, blocks=blocks, width=width),
        out_shape=jax.ShapeDtypeStruct((blocks, 2 * per + per // 2, width), bf16),
        in_specs=[vm] * 7,
        out_specs=vm,
        name="spectral",
    )(g, p, f, a_mat, at_mat, b_mat, tw)


def swap(x, axis):
    return lax.all_to_all(x, axis, split_axis=0, concat_axis=0, tiled=True)


def local(grad_out, out_weight, gate, key_in, value_in, conv_out, filt, skip_bias):
    channels, toks = gate.shape
    groups = lax.axis_size("ctx")
    parts = lax.axis_size("tp")
    per = channels // groups
    product = (key_in.astype(f32) * value_in.astype(f32)).astype(bf16)
    gated = (gate.astype(f32) * conv_out.astype(f32)).astype(bf16)
    spread = lax.optimization_barrier(jnp.broadcast_to(grad_out[None], (parts,) + grad_out.shape))
    grad_all = swap(spread, "tp").reshape(-1, toks)
    early = swap(
        jnp.concatenate([product.reshape(groups, per, toks), filt.reshape(groups, per, toks)], 1), "ctx"
    )
    grad_gated = jnp.dot(out_weight, grad_all, preferred_element_type=f32)
    gate_grad = (grad_gated * conv_out.astype(f32)).astype(bf16)
    conv_out_grad = (grad_gated * gate.astype(f32)).astype(bf16)
    g = swap(conv_out_grad.reshape(groups, per, toks), "ctx")
    weight_part = jnp.einsum(
        "it,qjt->qij", gated, grad_all.reshape(groups, -1, toks), preferred_element_type=f32
    ).astype(bf16)
    back = swap(spectral(g, early[:, :per], early[:, per:]), "ctx")
    weight_all = swap(weight_part, "ctx")
    weight_grad = jnp.sum(weight_all.astype(f32), axis=0)
    filter_grad = back[:, :per].reshape(channels, toks)
    conv_back = back[:, per : 2 * per].reshape(channels, toks)
    product_grad = (
        conv_back.astype(f32) + skip_bias[:, None] * conv_out_grad.astype(f32)
    ).astype(bf16)
    key_grad = (product_grad.astype(f32) * value_in.astype(f32)).astype(bf16)
    value_grad = (product_grad.astype(f32) * key_in.astype(f32)).astype(bf16)
    extra = back[:, 2 * per :].astype(f32).reshape(groups, per // 2, 4, toks // 4)[:, :, :, 0]
    sums = extra.reshape(groups, per // 2, 2, 2).sum(-1)
    bias_grad = sums.transpose(0, 2, 1).reshape(channels)
    return (gate_grad, key_grad, value_grad, filter_grad, weight_grad, bias_grad)


def solution(mesh):
    tok = P("tp", "ctx")
    return jax.shard_map(
        local,
        mesh=mesh,
        in_specs=(tok, P("tp", None), tok, tok, tok, tok, tok, P("tp")),
        out_specs=(tok, tok, tok, tok, tok, P("tp")),
        check_vma=False,
    )
```

```python
import functools

import jax
import jax.numpy as jnp
import numpy as np
from jax import lax
from jax.experimental import pallas as pl
from jax.experimental.pallas import tpu as pltpu
from jax.sharding import PartitionSpec as P

bf16 = jnp.bfloat16
f32 = jnp.float32
VM = pl.BlockSpec(memory_space=pltpu.VMEM)
SM = pl.BlockSpec(memory_space=pltpu.SMEM)


def hi_lo(table):
    high = table.astype(np.float32).astype(bf16)
    low = (table - high.astype(np.float64)).astype(np.float32).astype(bf16)
    return np.stack([high, low])


def dft_tables(blocks, per, width):
    full = 2 * blocks
    k = np.arange(full)[:, None]
    a = np.arange(blocks)[None, :]
    b = np.arange(width)
    outer = np.exp(-2j * np.pi * ((k * a) % full) / full)
    twist = np.exp(-2j * np.pi * ((k * b[None, :]) % (full * width)) / (full * width))
    inner = np.exp(-2j * np.pi * ((b[:, None] * b[None, :]) % width) / width)
    fwd = hi_lo(np.repeat(np.stack([outer.real, outer.imag]), per, axis=2))
    back = hi_lo(np.repeat(np.stack([outer.real.T, outer.imag.T]), per, axis=2))
    inner = hi_lo(np.concatenate([inner.real, inner.imag], 1))
    twist = np.stack([twist.real, twist.imag]).astype(np.float32)
    return jnp.asarray(fwd), jnp.asarray(back), jnp.asarray(inner), jnp.asarray(twist)


def dot(left, right):
    return jnp.dot(left, right, preferred_element_type=f32)


def split(x):
    high = x.astype(bf16)
    return high, (x - high.astype(f32)).astype(bf16)


def spread_rows(table, per):
    n, lanes = table.shape
    wide = jnp.broadcast_to(table.astype(f32)[:, None, :], (n, per, lanes))
    row = lax.broadcasted_iota(jnp.int32, (n, per, lanes), 1)
    lane = lax.broadcasted_iota(jnp.int32, (n, per, lanes), 2) % per
    return jnp.where(row == lane, wide, 0.0).reshape(n * per, lanes).astype(bf16)


def twisted(re, im, tw_ref, per, sign):
    n, width = tw_ref.shape[1:]
    re = re.reshape(n, per, width)
    im = im.reshape(n, per, width)
    tre = tw_ref[0][:, None, :]
    tim = tw_ref[1][:, None, :] * sign
    return (re * tre - im * tim).reshape(n * per, width), (re * tim + im * tre).reshape(n * per, width)


def inner_dft(re, im, b_ref, sign):
    width = b_ref.shape[1]
    bh = b_ref[0]
    bl = b_ref[1]

    def one(x):
        high, low = split(x)
        return dot(high, bh) + (dot(low, bh) + dot(high, bl))

    r = one(re)
    i = one(im)
    if sign > 0:
        return r[:, :width] - i[:, width:], r[:, width:] + i[:, :width]
    return r[:, :width] + i[:, width:], i[:, :width] - r[:, width:]


def prepare_kernel(early_ref, fwd_ref, back_ref, b_ref, tw_ref, z_ref, a_ref, at_ref, *, per, blocks, width):
    rows = 2 * blocks * per
    half = blocks * per
    for h in range(2):
        for c in range(2):
            a_ref[h, c * rows : (c + 1) * rows, :] = spread_rows(fwd_ref[h, c], per)
            at_ref[h, c] = spread_rows(back_ref[h, c], per)
    p = early_ref[:, :per, :].reshape(half, width)
    f = early_ref[:, per:, :].reshape(half, width)
    p1 = dot(a_ref[0], p) + dot(a_ref[1], p)
    f1 = dot(a_ref[0], f) + dot(a_ref[1], f)
    re, im = twisted(p1[:rows] + f1[rows:], p1[rows:] - f1[:rows], tw_ref, per, 1.0)
    re, im = inner_dft(re, im, b_ref, 1)
    z_ref[0] = re
    z_ref[1] = im


def spectral_kernel(g_ref, early_ref, z_ref, a_ref, at_ref, b_ref, tw_ref, out_ref, *, per, blocks, width):
    rows = 2 * blocks * per
    half = blocks * per
    g = g_ref[...].reshape(half, width)
    g1 = dot(a_ref[0], g) + dot(a_ref[1], g)
    re, im = twisted(g1[:rows], g1[rows:], tw_ref, per, 1.0)
    gre, gim = inner_dft(re, im, b_ref, 1)
    zre = z_ref[0]
    zim = z_ref[1]
    re, im = inner_dft(gre * zre + gim * zim, gim * zre - gre * zim, b_ref, -1)
    re, im = twisted(re, im, tw_ref, per, -1.0)
    scale = 1.0 / (2 * blocks * width)
    rh, rl = split(re * scale)
    ih, il = split(im * scale)

    def back(high, low, which):
        ah = at_ref[0, which]
        al = at_ref[1, which]
        return dot(ah, high) + (dot(al, high) + dot(ah, low))

    lag = back(rh, rl, 0) + back(ih, il, 1)
    conv = back(ih, il, 0) - back(rh, rl, 1)
    out_ref[:, :per, :] = lag.astype(bf16).reshape(blocks, per, width)
    out_ref[:, per : 2 * per, :] = conv.astype(bf16).reshape(blocks, per, width)
    prod = g_ref[...].astype(f32) * early_ref[:, :per, :].astype(f32)
    total = jnp.sum(jnp.sum(prod, axis=0), axis=1, keepdims=True)
    high = total.astype(bf16).astype(f32)
    low = total - high
    eighth = per // 2
    lane = lax.broadcasted_iota(jnp.int32, (eighth, width), 1) // (width // 4)
    top = jnp.where(lane == 0, high[:eighth], jnp.where(lane == 1, low[:eighth], 0.0))
    rest = jnp.where(lane == 2, high[eighth:], jnp.where(lane == 3, low[eighth:], 0.0))
    extra = (top + rest).astype(bf16)
    out_ref[:, 2 * per :, :] = jnp.broadcast_to(extra[None], (blocks, eighth, width))


def limit(mib):
    return pltpu.CompilerParams(vmem_limit_bytes=mib << 20)


def cost(flops, bytes_accessed):
    return pl.CostEstimate(flops=flops, bytes_accessed=bytes_accessed, transcendentals=0)


def prepare(early, tables):
    blocks, double, width = early.shape
    per = double // 2
    rows = 2 * blocks * per
    fwd, back, inner, twist = tables
    return pl.pallas_call(
        functools.partial(prepare_kernel, per=per, blocks=blocks, width=width),
        out_shape=(
            jax.ShapeDtypeStruct((2, rows, width), f32),
            jax.ShapeDtypeStruct((2, 2 * rows, blocks * per), bf16),
            jax.ShapeDtypeStruct((2, 2, blocks * per, rows), bf16),
        ),
        in_specs=[VM] * 5,
        out_specs=(VM, VM, VM),
        name="prepare",
        compiler_params=limit(20),
        cost_estimate=cost(2 * 12000 * 256 * 256, 4 << 20),
    )(early, fwd, back, inner, twist)


def spectral(g, early, spec, tables):
    blocks, per, width = g.shape
    z, a_mat, at_mat = spec
    return pl.pallas_call(
        functools.partial(spectral_kernel, per=per, blocks=blocks, width=width),
        out_shape=jax.ShapeDtypeStruct((blocks, 2 * per + per // 2, width), bf16),
        in_specs=[VM] * 7,
        out_specs=VM,
        name="spectral",
        compiler_params=limit(20),
        cost_estimate=cost(2 * 20000 * 256 * 256, 4 << 20),
    )(g, early, z, a_mat, at_mat, tables[2], tables[3])


def gated_kernel(order_ref, w_ref, gate_ref, conv_ref, *refs):
    blocks = refs[:-2]
    gate_grad_ref, grad_ref = refs[-2:]
    width = blocks[0].shape[0]
    total = jnp.zeros(grad_ref.shape, f32)
    for n, block in enumerate(blocks):
        columns = pl.ds(pl.multiple_of(order_ref[n] * width, width), width)
        total = total + dot(w_ref[:, columns], block[...])
    gate_grad_ref[...] = (total * conv_ref[...].astype(f32)).astype(bf16)
    grad_ref[...] = (total * gate_ref[...].astype(f32)).astype(bf16)


def gated_grads(order, weight, gate, conv_out, blocks):
    shape = jax.ShapeDtypeStruct(gate.shape, bf16)
    return pl.pallas_call(
        gated_kernel,
        out_shape=(shape, shape),
        in_specs=[SM] + [VM] * (3 + len(blocks)),
        out_specs=(VM, VM),
        name="gated_grads",
        compiler_params=limit(10),
        cost_estimate=cost(2 * gate.size * weight.shape[1], 5 << 20),
    )(order, weight, gate, conv_out, *blocks)


def weight_kernel(order_ref, gate_ref, conv_ref, *refs):
    blocks = refs[:-1]
    out_ref = refs[-1]
    gated = (gate_ref[...].astype(f32) * conv_ref[...].astype(f32)).astype(bf16)
    for n, block in enumerate(blocks):
        part = lax.dot_general(gated, block[...], (((1,), (1,)), ((), ())), preferred_element_type=f32)
        out_ref[order_ref[n]] = part.astype(bf16)


def weight_parts(order, gate, conv_out, blocks):
    return pl.pallas_call(
        weight_kernel,
        out_shape=jax.ShapeDtypeStruct((len(blocks),) + blocks[0].shape, bf16),
        in_specs=[SM] + [VM] * (2 + len(blocks)),
        out_specs=VM,
        name="weight_parts",
        compiler_params=limit(10),
        cost_estimate=cost(2 * gate.size * 4096, 4 << 20),
    )(order, gate, conv_out, *blocks)


def swap(x, axis):
    return lax.all_to_all(x, axis, split_axis=0, concat_axis=0, tiled=True)


def tp_moves():
    place = [(y, x, c) for y in range(4) for x in range(2) for c in range(2)]

    def index(y, x, c):
        return ((y % 4) * 2 + x) * 2 + c

    def step(d):
        return [(index(y, x, c), index(y + d, x, c)) for y, x, c in place]

    side = [(index(y, x, c), index(y, 1 - x, c)) for y, x, c in place]
    core = [(index(y, x, c), index(y, x, 1 - c)) for y, x, c in place]
    return step, side, core


def gather_tp(x):
    step, side, core = tp_moves()
    shifts = (0, 1, -1, 2)
    held = [x] + [lax.ppermute(x, "tp", step(d)) for d in shifts[1:]]
    held = held + [lax.ppermute(b, "tp", side) for b in held]
    held = held + [lax.ppermute(b, "tp", core) for b in held]
    order = [
        [(((y - d) % 4) * 2 + (xl ^ j)) * 2 + (c ^ i) for i in range(2) for j in range(2) for d in shifts]
        for y in range(4)
        for xl in range(2)
        for c in range(2)
    ]
    return held, jnp.asarray(np.array(order, np.int32))[lax.axis_index("tp")]


def local(grad_out, out_weight, gate, key_in, value_in, conv_out, filt, skip_bias):
    channels, toks = gate.shape
    groups = lax.axis_size("ctx")
    per = channels // groups
    product = (key_in.astype(f32) * value_in.astype(f32)).astype(bf16)
    early = swap(
        jnp.concatenate([product.reshape(groups, per, toks), filt.reshape(groups, per, toks)], 1), "ctx"
    )
    blocks, order = gather_tp(grad_out)
    gate_grad, conv_out_grad = gated_grads(order, out_weight, gate, conv_out, blocks)
    tables = dft_tables(groups, per, toks)
    spec = prepare(early, tables)
    g = swap(conv_out_grad.reshape(groups, per, toks), "ctx")
    weight_part = weight_parts(order, gate, conv_out, blocks)
    back = swap(spectral(g, early, spec, tables), "ctx")
    weight_all = swap(weight_part, "ctx")
    weight_grad = jnp.sum(weight_all.astype(f32), axis=0)
    filter_grad = back[:, :per].reshape(channels, toks)
    conv_back = back[:, per : 2 * per].reshape(channels, toks)
    product_grad = (
        conv_back.astype(f32) + skip_bias[:, None] * conv_out_grad.astype(f32)
    ).astype(bf16)
    key_grad = (product_grad.astype(f32) * value_in.astype(f32)).astype(bf16)
    value_grad = (product_grad.astype(f32) * key_in.astype(f32)).astype(bf16)
    extra = back[:, 2 * per :].astype(f32).reshape(groups, per // 2, 4, toks // 4)[:, :, :, 0]
    sums = extra.reshape(groups, per // 2, 2, 2).sum(-1)
    bias_grad = sums.transpose(0, 2, 1).reshape(channels)
    return (gate_grad, key_grad, value_grad, filter_grad, weight_grad, bias_grad)


def solution(mesh):
    tok = P("tp", "ctx")
    return jax.shard_map(
        local,
        mesh=mesh,
        in_specs=(tok, P("tp", None), tok, tok, tok, tok, tok, P("tp")),
        out_specs=(tok, tok, tok, tok, tok, P("tp")),
        check_vma=False,
    )
```

```python
import functools

import jax
import jax.numpy as jnp
import numpy as np
from jax import lax
from jax.experimental import pallas as pl
from jax.experimental.pallas import tpu as pltpu
from jax.sharding import PartitionSpec as P


bf16 = jnp.bfloat16
f32 = jnp.float32
VM = pl.BlockSpec(memory_space=pltpu.VMEM)
SM = pl.BlockSpec(memory_space=pltpu.SMEM)
HBM = pl.BlockSpec(memory_space=pltpu.HBM)


def hi_lo(table):
    high = table.astype(np.float32).astype(bf16)
    low = (table - high.astype(np.float64)).astype(np.float32).astype(bf16)
    return np.stack([high, low])


def dft_tables(blocks, per, width):
    full = 2 * blocks
    k = np.arange(full)[:, None]
    a = np.arange(blocks)[None, :]
    b = np.arange(width)
    outer = np.exp(-2j * np.pi * ((k * a) % full) / full)
    twist = np.exp(-2j * np.pi * ((k * b[None, :]) % (full * width)) / (full * width))
    inner = np.exp(-2j * np.pi * ((b[:, None] * b[None, :]) % width) / width)
    fwd = hi_lo(np.repeat(np.stack([outer.real, outer.imag]), per, axis=2))
    back = hi_lo(np.repeat(np.stack([outer.real.T, outer.imag.T]), per, axis=2))
    inner = hi_lo(np.concatenate([inner.real, inner.imag], 1))
    twist = np.stack([twist.real, twist.imag]).astype(np.float32)
    return jnp.asarray(fwd), jnp.asarray(back), jnp.asarray(inner), jnp.asarray(twist)


def dot(left, right):
    return jnp.dot(left, right, preferred_element_type=f32)


def split(x):
    high = x.astype(bf16)
    return high, (x - high.astype(f32)).astype(bf16)


def spread_rows(table, per):
    n, lanes = table.shape
    wide = jnp.broadcast_to(table.astype(f32)[:, None, :], (n, per, lanes))
    row = lax.broadcasted_iota(jnp.int32, (n, per, lanes), 1)
    lane = lax.broadcasted_iota(jnp.int32, (n, per, lanes), 2) % per
    return jnp.where(row == lane, wide, 0.0).reshape(n * per, lanes).astype(bf16)


def twisted(re, im, tw_ref, per, sign):
    n, width = tw_ref.shape[1:]
    re = re.reshape(n, per, width)
    im = im.reshape(n, per, width)
    tre = tw_ref[0][:, None, :]
    tim = tw_ref[1][:, None, :] * sign
    return (re * tre - im * tim).reshape(n * per, width), (re * tim + im * tre).reshape(n * per, width)


def inner_dft(re, im, b_ref, sign):
    width = b_ref.shape[1]
    bh = b_ref[0]
    bl = b_ref[1]

    def one(x):
        high, low = split(x)
        return dot(high, bh) + (dot(low, bh) + dot(high, bl))

    r = one(re)
    i = one(im)
    if sign > 0:
        return r[:, :width] - i[:, width:], r[:, width:] + i[:, :width]
    return r[:, :width] + i[:, width:], i[:, :width] - r[:, width:]


def outer_mat(fwd_ref, per):
    return [jnp.concatenate([spread_rows(fwd_ref[h, c], per) for c in range(2)], 0) for h in range(2)]


def prepare_kernel(early_ref, fwd_ref, b_ref, tw_ref, z_ref, *, per, blocks, width):
    rows = 2 * blocks * per
    half = blocks * per
    ah, al = outer_mat(fwd_ref, per)
    p = early_ref[:, :per, :].reshape(half, width)
    f = early_ref[:, per:, :].reshape(half, width)
    p1 = dot(ah, p) + dot(al, p)
    f1 = dot(ah, f) + dot(al, f)
    re, im = twisted(p1[:rows] + f1[rows:], p1[rows:] - f1[:rows], tw_ref, per, 1.0)
    re, im = inner_dft(re, im, b_ref, 1)
    z_ref[0] = re
    z_ref[1] = im


def spectral_kernel(
    g_ref, early_ref, z_hbm, fwd_ref, back_ref, b_ref, tw_ref, out_ref, z_ref, sem, *, per, blocks, width
):
    fetch = pltpu.make_async_copy(z_hbm, z_ref, sem)
    fetch.start()
    rows = 2 * blocks * per
    half = blocks * per
    g = g_ref[...].reshape(half, width)
    ah, al = outer_mat(fwd_ref, per)
    g1 = dot(ah, g) + dot(al, g)
    re, im = twisted(g1[:rows], g1[rows:], tw_ref, per, 1.0)
    gre, gim = inner_dft(re, im, b_ref, 1)
    fetch.wait()
    zre = z_ref[0]
    zim = z_ref[1]
    re, im = inner_dft(gre * zre + gim * zim, gim * zre - gre * zim, b_ref, -1)
    re, im = twisted(re, im, tw_ref, per, -1.0)
    scale = 1.0 / (2 * blocks * width)
    rh, rl = split(re * scale)
    ih, il = split(im * scale)
    mats = [[spread_rows(back_ref[h, c], per) for c in range(2)] for h in range(2)]

    def back(high, low, which):
        return dot(mats[0][which], high) + (dot(mats[1][which], high) + dot(mats[0][which], low))

    lag = back(rh, rl, 0) + back(ih, il, 1)
    conv = back(ih, il, 0) - back(rh, rl, 1)
    out_ref[:, :per, :] = lag.astype(bf16).reshape(blocks, per, width)
    out_ref[:, per : 2 * per, :] = conv.astype(bf16).reshape(blocks, per, width)
    prod = g_ref[...].astype(f32) * early_ref[:, :per, :].astype(f32)
    total = jnp.sum(jnp.sum(prod, axis=0), axis=1, keepdims=True)
    row = lax.broadcasted_iota(jnp.int32, (per, width), 0)
    lane = lax.broadcasted_iota(jnp.int32, (per, width), 1) % per
    total = jnp.sum(jnp.where(row == lane, total, 0.0), axis=0, keepdims=True)
    high = total.astype(bf16).astype(f32)
    eighth = per // 2
    which = lax.broadcasted_iota(jnp.int32, (eighth, width), 0)
    extra = jnp.where(which == 0, high, jnp.where(which == 1, total - high, 0.0)).astype(bf16)
    out_ref[:, 2 * per :, :] = jnp.broadcast_to(extra[None], (blocks, eighth, width))


def limit(mib):
    return pltpu.CompilerParams(vmem_limit_bytes=mib << 20)


def cost(flops, bytes_accessed):
    return pl.CostEstimate(flops=flops, bytes_accessed=bytes_accessed, transcendentals=0)


def prepare(early, tables):
    blocks, double, width = early.shape
    per = double // 2
    rows = 2 * blocks * per
    fwd, _, inner, twist = tables
    return pl.pallas_call(
        functools.partial(prepare_kernel, per=per, blocks=blocks, width=width),
        out_shape=jax.ShapeDtypeStruct((2, rows, width), f32),
        in_specs=[VM] * 4,
        out_specs=VM,
        name="prepare",
        compiler_params=limit(20),
        cost_estimate=cost(2 * 12000 * 256 * 256, 4 << 20),
    )(early, fwd, inner, twist)


def spectral(g, early, z, tables):
    blocks, per, width = g.shape
    return pl.pallas_call(
        functools.partial(spectral_kernel, per=per, blocks=blocks, width=width),
        out_shape=jax.ShapeDtypeStruct((blocks, 2 * per + per // 2, width), bf16),
        in_specs=[VM, VM, HBM] + [VM] * 4,
        out_specs=VM,
        scratch_shapes=[pltpu.VMEM(z.shape, f32), pltpu.SemaphoreType.DMA],
        name="spectral",
        compiler_params=limit(24),
        cost_estimate=cost(2 * 20000 * 256 * 256, 4 << 20),
    )(g, early, z, *tables)


def gated_kernel(order_ref, w_hbm, gate_hbm, conv_hbm, own_hbm, *refs):
    blocks = list(refs[:-7])
    gate_grad_ref, grad_ref, w_ref, gate_ref, conv_ref, own_ref, sems = refs[-7:]
    width = grad_ref.shape[1]
    pairs = ((own_hbm, own_ref), (w_hbm, w_ref), (gate_hbm, gate_ref), (conv_hbm, conv_ref))
    copies = [pltpu.make_async_copy(src, dst, sems.at[n]) for n, (src, dst) in enumerate(pairs)]
    for copy in copies:
        copy.start()
    copies[0].wait()
    copies[1].wait()
    total = jnp.zeros(grad_ref.shape, f32)
    for n, block in enumerate([own_ref] + blocks):
        columns = pl.ds(pl.multiple_of(order_ref[n] * width, width), width)
        total = total + dot(w_ref[:, columns], block[...])
    copies[2].wait()
    copies[3].wait()
    gate_grad_ref[...] = (total * conv_ref[...].astype(f32)).astype(bf16)
    grad_ref[...] = (total * gate_ref[...].astype(f32)).astype(bf16)


def gated_grads(order, weight, gate, conv_out, blocks):
    shape = jax.ShapeDtypeStruct(gate.shape, bf16)
    small = pltpu.VMEM(gate.shape, bf16)
    return pl.pallas_call(
        gated_kernel,
        out_shape=(shape, shape),
        in_specs=[SM] + [HBM] * 4 + [VM] * (len(blocks) - 1),
        out_specs=(VM, VM),
        scratch_shapes=[pltpu.VMEM(weight.shape, bf16), small, small, small, pltpu.SemaphoreType.DMA((4,))],
        name="gated_grads",
        compiler_params=limit(6),
        cost_estimate=cost(2 * gate.size * weight.shape[1], 5 << 20),
    )(order, weight, gate, conv_out, *blocks)


def pack_kernel(order_ref, pick_ref, gate_hbm, conv_hbm, own_hbm, after_hbm, *refs):
    blocks = list(refs[:-9])
    side_ref, down_ref, cross_ref, mine_ref, sorted_ref, gate_ref, conv_ref, own_ref, sems = refs[-9:]
    pairs = ((own_hbm, own_ref), (gate_hbm, gate_ref), (conv_hbm, conv_ref))
    copies = [pltpu.make_async_copy(src, dst, sems.at[n]) for n, (src, dst) in enumerate(pairs)]
    for copy in copies:
        copy.start()
    for n, block in enumerate(blocks):
        sorted_ref[order_ref[n + 1]] = block[...]
    for copy in copies:
        copy.wait()
    sorted_ref[order_ref[0]] = own_ref[...]
    gated = (gate_ref[...].astype(f32) * conv_ref[...].astype(f32)).astype(bf16)
    for m, out in enumerate((side_ref, down_ref, cross_ref)):
        for i in range(2):
            out[i] = sorted_ref[pick_ref[2 * m + i]]
        out[2] = gated
    for r in range(4):
        mine_ref[r] = sorted_ref[pick_ref[6 + r]]
    mine_ref[4] = gated


def pack(order, pick, gate, conv_out, blocks, after):
    shape = gate.shape
    small = pltpu.VMEM(shape, bf16)
    return pl.pallas_call(
        pack_kernel,
        out_shape=tuple(jax.ShapeDtypeStruct((n,) + shape, bf16) for n in (3, 3, 3, 5)),
        in_specs=[SM, SM] + [HBM] * 4 + [VM] * (len(blocks) - 1),
        out_specs=(VM,) * 4,
        scratch_shapes=[
            pltpu.VMEM((len(blocks),) + shape, bf16),
            small,
            small,
            small,
            pltpu.SemaphoreType.DMA((3,)),
        ],
        name="pack",
        compiler_params=limit(8),
        cost_estimate=cost(gate.size, 4 << 20),
    )(order, pick, gate, conv_out, blocks[0], after, *blocks[1:])


def weight_kernel(pick_ref, mine_ref, *refs):
    received = refs[:3]
    swapped = refs[3:6]
    own_ref, one_ref, two_ref, three_ref, sum_ref = refs[-5:]

    def outer(rows, block):
        return lax.dot_general(rows, block, (((1,), (1,)), ((), ())), preferred_element_type=f32)

    rows = [mine_ref[4]] + [ref[2] for ref in received]
    core = pick_ref[10]
    for half, source in ((core, received), (1 - core, swapped)):
        for i in range(2):
            r = 2 * half + i
            total = outer(rows[0], mine_ref[r])
            for m in range(3):
                total = total + outer(rows[m + 1], source[m][i])
            sum_ref[r] = total
    own_ref[...] = sum_ref[pick_ref[11]]
    for d, out in enumerate((one_ref, two_ref, three_ref)):
        out[...] = sum_ref[pick_ref[12 + d]].astype(bf16)


def weight_parts(pick, mine, received, swapped, after):
    shape = mine.shape[1:]
    part = jax.ShapeDtypeStruct(shape, bf16)
    return pl.pallas_call(
        weight_kernel_after,
        out_shape=(jax.ShapeDtypeStruct(shape, f32), part, part, part),
        in_specs=[SM, HBM] + [VM] * 7,
        out_specs=(VM,) * 4,
        scratch_shapes=[pltpu.VMEM((4,) + shape, f32)],
        name="weight_parts",
        compiler_params=limit(8),
        cost_estimate=cost(2 * 16 * 256 * 256 * 256, 4 << 20),
    )(pick, after, mine, *received, *swapped)


def weight_kernel_after(pick_ref, after_hbm, *refs):
    weight_kernel(pick_ref, *refs)


def final_kernel(back_ref, grad_ref, key_ref, value_ref, skip_ref, filter_ref, dkey_ref, dvalue_ref, bias_ref, *, per):
    groups, _, width = back_ref.shape
    channels = groups * per
    filter_ref[...] = back_ref[:, :per, :].reshape(channels, width)
    conv = back_ref[:, per : 2 * per, :].reshape(channels, width).astype(f32)
    total = (conv + skip_ref[...] * grad_ref[...].astype(f32)).astype(bf16).astype(f32)
    dkey_ref[...] = (total * value_ref[...].astype(f32)).astype(bf16)
    dvalue_ref[...] = (total * key_ref[...].astype(f32)).astype(bf16)
    extra = back_ref[:, 2 * per :, :].astype(f32)
    pair = extra[:, 0, :] + extra[:, 1, :]
    row = lax.broadcasted_iota(jnp.int32, (groups, width), 0)
    lane = lax.broadcasted_iota(jnp.int32, (groups, width), 1) // per
    bias_ref[...] = jnp.sum(jnp.where(row == lane, pair, 0.0), axis=0, keepdims=True)


def final(back, grad, key_in, value_in, skip_bias):
    shape = jax.ShapeDtypeStruct(key_in.shape, bf16)
    channels = key_in.shape[0]
    per = channels // back.shape[0]
    return pl.pallas_call(
        functools.partial(final_kernel, per=per),
        out_shape=(shape, shape, shape, jax.ShapeDtypeStruct((1, channels), f32)),
        in_specs=[VM] * 5,
        out_specs=(VM,) * 4,
        name="final",
        compiler_params=limit(6),
        cost_estimate=cost(8 * key_in.size, 1 << 20),
    )(back, grad, key_in, value_in, skip_bias[:, None])


def swap(x, axis):
    return lax.all_to_all(x, axis, split_axis=0, concat_axis=0, tiled=True)


def tp_moves():
    place = [(y, x, c) for y in range(4) for x in range(2) for c in range(2)]

    def index(y, x, c):
        return ((y % 4) * 2 + x) * 2 + c

    def step(d):
        return [(index(y, x, c), index(y + d, x, c)) for y, x, c in place]

    side = [(index(y, x, c), index(y, 1 - x, c)) for y, x, c in place]
    core = [(index(y, x, c), index(y, x, 1 - c)) for y, x, c in place]
    return step, side, core


def gather_tp(x):
    step, side, core = tp_moves()
    shifts = (0, 1, -1, 2)
    held = [x]
    for d in shifts[1:]:
        held.append(lax.ppermute(x, "tp", step(d)))
    held = held + [lax.ppermute(b, "tp", side) for b in held]
    held = held + [lax.ppermute(b, "tp", core) for b in held]
    order = [
        [(((y - d) % 4) * 2 + (xl ^ j)) * 2 + (c ^ i) for i in range(2) for j in range(2) for d in shifts]
        for y in range(4)
        for xl in range(2)
        for c in range(2)
    ]
    return held, jnp.asarray(np.array(order, np.int32))[lax.axis_index("tp")]


def weight_moves():
    place = [(z, h) for z in range(8) for h in range(2)]
    side = [(z * 2 + h, z * 2 + 1 - h) for z, h in place]
    down = [(z * 2 + h, (z ^ 1) * 2 + h) for z, h in place]
    cross = [(z * 2 + h, (z ^ 1) * 2 + 1 - h) for z, h in place]
    ahead = [[(z * 2 + h, ((z + 2 * d) % 8) * 2 + h) for z, h in place] for d in (1, 2, 3)]
    pick = np.zeros((16, 2, 16), np.int32)
    for z, h in place:
        for k in range(2):
            row = []
            for zz, hh in ((z, 1 - h), (z ^ 1, h), (z ^ 1, 1 - h)):
                row += [(zz % 2 + 2 * (2 * k + i)) * 2 + hh for i in range(2)]
            row += [(z % 2 + 2 * r) * 2 + h for r in range(4)]
            row += [k] + [(z // 2 + d) % 4 for d in range(4)]
            pick[z * 2 + h, k, : len(row)] = row
    pick = jnp.asarray(pick)[lax.axis_index("ctx"), lax.axis_index("tp") % 2]
    return (side, down, cross), ahead, pick


def local(grad_out, out_weight, gate, key_in, value_in, conv_out, filt, skip_bias):
    channels, toks = gate.shape
    groups = lax.axis_size("ctx")
    per = channels // groups
    product = (key_in.astype(f32) * value_in.astype(f32)).astype(bf16)
    early = swap(
        jnp.concatenate([product.reshape(groups, per, toks), filt.reshape(groups, per, toks)], 1), "ctx"
    )
    blocks, order = gather_tp(grad_out)
    near, ahead, pick = weight_moves()
    gate_grad, conv_out_grad = gated_grads(order, out_weight, gate, conv_out, blocks)
    tables = dft_tables(groups, per, toks)
    z = prepare(early, tables)
    g = swap(conv_out_grad.reshape(groups, per, toks), "ctx")
    *messages, mine = pack(order, pick, gate, conv_out, blocks, conv_out_grad)
    received = []
    for message, move in zip(messages, near):
        received.append(lax.ppermute(message, "ctx", move))
    core = tp_moves()[2]
    swapped = []
    for r in received:
        swapped.append(lax.ppermute(r, "tp", core))
    result = spectral(g, early, z, tables)
    back = swap(result, "ctx")
    weight_grad, *parts = weight_parts(pick, mine, received, swapped, result)
    for part, move in zip(parts, ahead):
        weight_grad = weight_grad + lax.ppermute(part, "ctx", move).astype(f32)
    filter_grad, key_grad, value_grad, bias_grad = final(back, conv_out_grad, key_in, value_in, skip_bias)
    return (gate_grad, key_grad, value_grad, filter_grad, weight_grad, bias_grad.reshape(channels))


def solution(mesh):
    tok = P("tp", "ctx")
    return jax.shard_map(
        local,
        mesh=mesh,
        in_specs=(tok, P("tp", None), tok, tok, tok, tok, tok, P("tp")),
        out_specs=(tok, tok, tok, tok, tok, P("tp")),
        check_vma=False,
    )
```

```python
import functools

import jax
import jax.numpy as jnp
import numpy as np
from jax import lax
from jax.experimental import pallas as pl
from jax.experimental.pallas import tpu as pltpu
from jax.sharding import PartitionSpec as P


bf16 = jnp.bfloat16
f32 = jnp.float32
VM = pl.BlockSpec(memory_space=pltpu.VMEM)
SM = pl.BlockSpec(memory_space=pltpu.SMEM)
HBM = pl.BlockSpec(memory_space=pltpu.HBM)


def hi_lo(table):
    high = table.astype(np.float32).astype(bf16)
    low = (table - high.astype(np.float64)).astype(np.float32).astype(bf16)
    return np.stack([high, low])


def dft_tables(blocks, per, width):
    full = 2 * blocks
    k = np.arange(full)[:, None]
    a = np.arange(blocks)[None, :]
    b = np.arange(width)
    outer = np.exp(-2j * np.pi * ((k * a) % full) / full)
    twist = np.exp(-2j * np.pi * ((k * b[None, :]) % (full * width)) / (full * width))
    inner = np.exp(-2j * np.pi * ((b[:, None] * b[None, :]) % width) / width)
    fwd = hi_lo(np.repeat(np.stack([outer.real, outer.imag]), per, axis=2))
    back = hi_lo(np.repeat(np.stack([outer.real.T, outer.imag.T]), per, axis=2))
    inner = hi_lo(np.concatenate([inner.real, inner.imag], 1))
    twist = np.stack([twist.real, twist.imag]).astype(np.float32)
    return jnp.asarray(fwd), jnp.asarray(back), jnp.asarray(inner), jnp.asarray(twist)


def dot(left, right):
    return jnp.dot(left, right, preferred_element_type=f32)


def split(x):
    high = x.astype(bf16)
    return high, (x - high.astype(f32)).astype(bf16)


def spread_rows(table, per):
    n, lanes = table.shape
    wide = jnp.broadcast_to(table.astype(f32)[:, None, :], (n, per, lanes))
    row = lax.broadcasted_iota(jnp.int32, (n, per, lanes), 1)
    lane = lax.broadcasted_iota(jnp.int32, (n, per, lanes), 2) % per
    return jnp.where(row == lane, wide, 0.0).reshape(n * per, lanes).astype(bf16)


def twisted(re, im, tw_ref, per, sign):
    n, width = tw_ref.shape[1:]
    re = re.reshape(n, per, width)
    im = im.reshape(n, per, width)
    tre = tw_ref[0][:, None, :]
    tim = tw_ref[1][:, None, :] * sign
    return (re * tre - im * tim).reshape(n * per, width), (re * tim + im * tre).reshape(n * per, width)


def inner_dft(re, im, b_ref, sign):
    width = b_ref.shape[1]
    bh = b_ref[0]
    bl = b_ref[1]

    def one(x):
        high, low = split(x)
        return dot(high, bh) + (dot(low, bh) + dot(high, bl))

    r = one(re)
    i = one(im)
    if sign > 0:
        return r[:, :width] - i[:, width:], r[:, width:] + i[:, :width]
    return r[:, :width] + i[:, width:], i[:, :width] - r[:, width:]


def spectral_kernel(msg_ref, *refs, per, blocks, width):
    sources, out_ref, (fwd_ref, back_ref, b_ref, tw_ref), sems = refs[:4], refs[4], refs[5:9], refs[9]
    copies = [pltpu.make_async_copy(src, dst, sems.at[n]) for n, (src, dst) in enumerate(zip(sources, refs[5:9]))]
    for n in (0, 3, 2, 1):
        copies[n].start()
    copies[0].wait()
    rows = 2 * blocks * per
    half = blocks * per
    g, p, f = [msg_ref[:, n * per : (n + 1) * per, :].reshape(half, width) for n in range(3)]
    high, low = [
        jnp.concatenate([spread_rows(fwd_ref[h, c], per) for c in range(2)], 0) for h in range(2)
    ]
    g1, p1, f1 = [dot(high, x) + dot(low, x) for x in (g, p, f)]
    copies[3].wait()
    copies[2].wait()
    gre, gim = inner_dft(*twisted(g1[:rows], g1[rows:], tw_ref, per, 1.0), b_ref, 1)
    zre, zim = inner_dft(*twisted(p1[:rows] + f1[rows:], p1[rows:] - f1[:rows], tw_ref, per, 1.0), b_ref, 1)
    re, im = inner_dft(gre * zre + gim * zim, gim * zre - gre * zim, b_ref, -1)
    re, im = twisted(re, im, tw_ref, per, -1.0)
    scale = 1.0 / (2 * blocks * width)
    rh, rl = split(re * scale)
    ih, il = split(im * scale)
    copies[1].wait()
    mats = [[spread_rows(back_ref[h, c], per) for c in range(2)] for h in range(2)]

    def back(high, low, which):
        return dot(mats[0][which], high) + (dot(mats[1][which], high) + dot(mats[0][which], low))

    lag = back(rh, rl, 0) + back(ih, il, 1)
    conv = back(ih, il, 0) - back(rh, rl, 1)
    out_ref[:, :per, :] = lag.astype(bf16).reshape(blocks, per, width)
    out_ref[:, per : 2 * per, :] = conv.astype(bf16).reshape(blocks, per, width)
    prod = (g.astype(f32) * p.astype(f32)).reshape(blocks, per, width)
    total = jnp.sum(jnp.sum(prod, axis=0), axis=1, keepdims=True)
    row = lax.broadcasted_iota(jnp.int32, (per, width), 0)
    lane = lax.broadcasted_iota(jnp.int32, (per, width), 1) % per
    total = jnp.sum(jnp.where(row == lane, total, 0.0), axis=0, keepdims=True)
    high = total.astype(bf16).astype(f32)
    eighth = per // 2
    which = lax.broadcasted_iota(jnp.int32, (eighth, width), 0)
    extra = jnp.where(which == 0, high, jnp.where(which == 1, total - high, 0.0)).astype(bf16)
    out_ref[:, 2 * per :, :] = jnp.broadcast_to(extra[None], (blocks, eighth, width))


def in_hbm(x):
    return pltpu.with_memory_space_constraint(x, pltpu.HBM)


def limit(mib):
    return pltpu.CompilerParams(vmem_limit_bytes=mib << 20)


def cost(flops, bytes_accessed):
    return pl.CostEstimate(flops=flops, bytes_accessed=bytes_accessed, transcendentals=0)


def spectral(msg, tables):
    blocks, triple, width = msg.shape
    per = triple // 3
    return pl.pallas_call(
        functools.partial(spectral_kernel, per=per, blocks=blocks, width=width),
        out_shape=jax.ShapeDtypeStruct((blocks, 2 * per + per // 2, width), bf16),
        in_specs=[VM] + [HBM] * 4,
        out_specs=VM,
        scratch_shapes=[pltpu.VMEM(t.shape, t.dtype) for t in tables] + [pltpu.SemaphoreType.DMA((4,))],
        name="spectral",
        compiler_params=limit(28),
        cost_estimate=cost(2 * 32000 * 256 * 256, 2 << 20),
    )(msg, *[in_hbm(t) for t in tables])


def gated_kernel(order_ref, *refs, per):
    sources = refs[:7]
    gate_grad_ref, msg_ref = refs[-10:-8]
    blocks = list(refs[7:-10])
    buffers, sems = refs[-8:-1], refs[-1]
    copies = [pltpu.make_async_copy(src, dst, sems.at[n]) for n, (src, dst) in enumerate(zip(sources, buffers))]
    for copy in copies:
        copy.start()
    own_ref, w_ref, gate_ref, conv_ref, key_ref, value_ref, filt_ref = buffers
    groups, _, width = msg_ref.shape
    for n in (4, 5, 6, 0, 1):
        copies[n].wait()
    product = (key_ref[...].astype(f32) * value_ref[...].astype(f32)).astype(bf16)
    msg_ref[:, per : 2 * per, :] = product.reshape(groups, per, width)
    msg_ref[:, 2 * per :, :] = filt_ref[...].reshape(groups, per, width)
    total = jnp.zeros(gate_grad_ref.shape, f32)
    for n, block in enumerate([own_ref] + blocks):
        columns = pl.ds(pl.multiple_of(order_ref[n] * width, width), width)
        total = total + dot(w_ref[:, columns], block[...])
    copies[2].wait()
    copies[3].wait()
    gate_grad_ref[...] = (total * conv_ref[...].astype(f32)).astype(bf16)
    msg_ref[:, :per, :] = (total * gate_ref[...].astype(f32)).astype(bf16).reshape(groups, per, width)


def gated_grads(order, weight, gate, conv_out, key_in, value_in, filt, blocks, groups):
    channels, width = gate.shape
    per = channels // groups
    small = pltpu.VMEM(gate.shape, bf16)
    held = [blocks[0], weight, gate, conv_out, key_in, value_in, filt]
    return pl.pallas_call(
        functools.partial(gated_kernel, per=per),
        out_shape=(
            jax.ShapeDtypeStruct(gate.shape, bf16),
            jax.ShapeDtypeStruct((groups, 3 * per, width), bf16),
        ),
        in_specs=[SM] + [HBM] * 7 + [VM] * (len(blocks) - 1),
        out_specs=(VM, VM),
        scratch_shapes=[small, pltpu.VMEM(weight.shape, bf16)] + [small] * 5 + [pltpu.SemaphoreType.DMA((7,))],
        name="gated_grads",
        compiler_params=limit(6),
        cost_estimate=cost(2 * gate.size * weight.shape[1], 5 << 20),
    )(order, *[in_hbm(x) for x in held], *blocks[1:])


def pack_kernel(order_ref, pick_ref, gate_hbm, conv_hbm, own_hbm, after_hbm, *refs):
    blocks = list(refs[:-9])
    side_ref, down_ref, cross_ref, mine_ref, sorted_ref, gate_ref, conv_ref, own_ref, sems = refs[-9:]
    pairs = ((own_hbm, own_ref), (gate_hbm, gate_ref), (conv_hbm, conv_ref))
    copies = [pltpu.make_async_copy(src, dst, sems.at[n]) for n, (src, dst) in enumerate(pairs)]
    for copy in copies:
        copy.start()
    for n, block in enumerate(blocks):
        sorted_ref[order_ref[n + 1]] = block[...]
    for copy in copies:
        copy.wait()
    sorted_ref[order_ref[0]] = own_ref[...]
    gated = (gate_ref[...].astype(f32) * conv_ref[...].astype(f32)).astype(bf16)
    for m, out in enumerate((side_ref, down_ref, cross_ref)):
        for i in range(2):
            out[i] = sorted_ref[pick_ref[2 * m + i]]
        out[2] = gated
    for r in range(4):
        mine_ref[r] = sorted_ref[pick_ref[6 + r]]
    mine_ref[4] = gated


def pack(order, pick, gate, conv_out, blocks, after):
    shape = gate.shape
    small = pltpu.VMEM(shape, bf16)
    return pl.pallas_call(
        pack_kernel,
        out_shape=tuple(jax.ShapeDtypeStruct((n,) + shape, bf16) for n in (3, 3, 3, 5)),
        in_specs=[SM, SM] + [HBM] * 4 + [VM] * (len(blocks) - 1),
        out_specs=(VM,) * 4,
        scratch_shapes=[
            pltpu.VMEM((len(blocks),) + shape, bf16),
            small,
            small,
            small,
            pltpu.SemaphoreType.DMA((3,)),
        ],
        name="pack",
        compiler_params=limit(8),
        cost_estimate=cost(gate.size, 4 << 20),
    )(order, pick, in_hbm(gate), in_hbm(conv_out), in_hbm(blocks[0]), after, *blocks[1:])


def weight_kernel(pick_ref, mine_ref, *refs):
    received = refs[:3]
    swapped = refs[3:6]
    own_ref, one_ref, two_ref, three_ref, sum_ref = refs[-5:]

    def outer(rows, block):
        return lax.dot_general(rows, block, (((1,), (1,)), ((), ())), preferred_element_type=f32)

    rows = [mine_ref[4]] + [ref[2] for ref in received]
    core = pick_ref[10]
    for half, source in ((core, received), (1 - core, swapped)):
        for i in range(2):
            r = 2 * half + i
            total = outer(rows[0], mine_ref[r])
            for m in range(3):
                total = total + outer(rows[m + 1], source[m][i])
            sum_ref[r] = total
    own_ref[...] = sum_ref[pick_ref[11]]
    for d, out in enumerate((one_ref, two_ref, three_ref)):
        out[...] = sum_ref[pick_ref[12 + d]].astype(bf16)


def weight_parts(pick, mine, received, swapped, after):
    shape = mine.shape[1:]
    part = jax.ShapeDtypeStruct(shape, bf16)
    return pl.pallas_call(
        weight_kernel_after,
        out_shape=(jax.ShapeDtypeStruct(shape, f32), part, part, part),
        in_specs=[SM, HBM] + [VM] * 7,
        out_specs=(VM,) * 4,
        scratch_shapes=[pltpu.VMEM((4,) + shape, f32)],
        name="weight_parts",
        compiler_params=limit(8),
        cost_estimate=cost(2 * 16 * 256 * 256 * 256, 4 << 20),
    )(pick, after, mine, *received, *swapped)


def weight_kernel_after(pick_ref, after_hbm, *refs):
    weight_kernel(pick_ref, *refs)


def final_kernel(back_ref, msg_ref, key_ref, value_ref, skip_ref, filter_ref, dkey_ref, dvalue_ref, bias_ref, *, per):
    groups, _, width = back_ref.shape
    channels = groups * per
    filter_ref[...] = back_ref[:, :per, :].reshape(channels, width)
    conv = back_ref[:, per : 2 * per, :].reshape(channels, width).astype(f32)
    grad = msg_ref[:, :per, :].reshape(channels, width).astype(f32)
    total = (conv + skip_ref[...] * grad).astype(bf16).astype(f32)
    dkey_ref[...] = (total * value_ref[...].astype(f32)).astype(bf16)
    dvalue_ref[...] = (total * key_ref[...].astype(f32)).astype(bf16)
    extra = back_ref[:, 2 * per :, :].astype(f32)
    pair = extra[:, 0, :] + extra[:, 1, :]
    row = lax.broadcasted_iota(jnp.int32, (groups, width), 0)
    lane = lax.broadcasted_iota(jnp.int32, (groups, width), 1) // per
    bias_ref[...] = jnp.sum(jnp.where(row == lane, pair, 0.0), axis=0, keepdims=True)


def final(back, msg, key_in, value_in, skip_bias):
    shape = jax.ShapeDtypeStruct(key_in.shape, bf16)
    channels = key_in.shape[0]
    per = channels // back.shape[0]
    return pl.pallas_call(
        functools.partial(final_kernel, per=per),
        out_shape=(shape, shape, shape, jax.ShapeDtypeStruct((1, channels), f32)),
        in_specs=[VM] * 5,
        out_specs=(VM,) * 4,
        name="final",
        compiler_params=limit(6),
        cost_estimate=cost(8 * key_in.size, 1 << 20),
    )(back, msg, key_in, value_in, skip_bias[:, None])


def sum_kernel(after_hbm, own_ref, one_ref, two_ref, three_ref, out_ref):
    total = own_ref[...] + one_ref[...].astype(f32)
    out_ref[...] = total + (two_ref[...].astype(f32) + three_ref[...].astype(f32))


def sum_parts(own, parts, after):
    return pl.pallas_call(
        sum_kernel,
        out_shape=jax.ShapeDtypeStruct(own.shape, f32),
        in_specs=[HBM] + [VM] * 4,
        out_specs=VM,
        name="sum_parts",
        compiler_params=limit(3),
        cost_estimate=cost(4 * own.size, 1 << 20),
    )(in_hbm(after), own, *parts)


def swap(x, axis):
    return lax.all_to_all(x, axis, split_axis=0, concat_axis=0, tiled=True)


def tp_moves():
    place = [(y, x, c) for y in range(4) for x in range(2) for c in range(2)]

    def index(y, x, c):
        return ((y % 4) * 2 + x) * 2 + c

    def step(d):
        return [(index(y, x, c), index(y + d, x, c)) for y, x, c in place]

    side = [(index(y, x, c), index(y, 1 - x, c)) for y, x, c in place]
    core = [(index(y, x, c), index(y, x, 1 - c)) for y, x, c in place]
    return step, side, core


def gather_tp(x):
    step, side, core = tp_moves()
    shifts = (0, 1, -1, 2)
    held = [x]
    for d in shifts[1:]:
        held.append(lax.ppermute(x, "tp", step(d)))
    held = held + [lax.ppermute(b, "tp", side) for b in held]
    held = held + [lax.ppermute(b, "tp", core) for b in held]
    order = [
        [(((y - d) % 4) * 2 + (xl ^ j)) * 2 + (c ^ i) for i in range(2) for j in range(2) for d in shifts]
        for y in range(4)
        for xl in range(2)
        for c in range(2)
    ]
    return held, jnp.asarray(np.array(order, np.int32))[lax.axis_index("tp")]


def weight_moves():
    place = [(z, h) for z in range(8) for h in range(2)]
    side = [(z * 2 + h, z * 2 + 1 - h) for z, h in place]
    down = [(z * 2 + h, (z ^ 1) * 2 + h) for z, h in place]
    cross = [(z * 2 + h, (z ^ 1) * 2 + 1 - h) for z, h in place]
    ahead = [[(z * 2 + h, ((z + 2 * d) % 8) * 2 + h) for z, h in place] for d in (1, 2, 3)]
    pick = np.zeros((16, 2, 16), np.int32)
    for z, h in place:
        for k in range(2):
            row = []
            for zz, hh in ((z, 1 - h), (z ^ 1, h), (z ^ 1, 1 - h)):
                row += [(zz % 2 + 2 * (2 * k + i)) * 2 + hh for i in range(2)]
            row += [(z % 2 + 2 * r) * 2 + h for r in range(4)]
            row += [k] + [(z // 2 + d) % 4 for d in range(4)]
            pick[z * 2 + h, k, : len(row)] = row
    pick = jnp.asarray(pick)[lax.axis_index("ctx"), lax.axis_index("tp") % 2]
    return (side, down, cross), ahead, pick


def local(grad_out, out_weight, gate, key_in, value_in, conv_out, filt, skip_bias):
    channels, toks = gate.shape
    groups = lax.axis_size("ctx")
    per = channels // groups
    blocks, order = gather_tp(grad_out)
    near, ahead, pick = weight_moves()
    gate_grad, msg = gated_grads(order, out_weight, gate, conv_out, key_in, value_in, filt, blocks, groups)
    whole = swap(msg, "ctx")
    *messages, mine = pack(order, pick, gate, conv_out, blocks, msg)
    received = []
    for message, move in zip(messages, near):
        received.append(lax.ppermute(message, "ctx", move))
    core = tp_moves()[2]
    swapped = []
    for r in received:
        swapped.append(lax.ppermute(r, "tp", core))
    result = spectral(whole, dft_tables(groups, per, toks))
    back = swap(result, "ctx")
    own, *parts = weight_parts(pick, mine, received, swapped, result)
    for n, move in enumerate(ahead):
        parts[n] = lax.ppermute(parts[n], "ctx", move)
    filter_grad, key_grad, value_grad, bias_grad = final(back, msg, key_in, value_in, skip_bias)
    weight_grad = sum_parts(own, parts, filter_grad)
    return (gate_grad, key_grad, value_grad, filter_grad, weight_grad, bias_grad.reshape(channels))


def solution(mesh):
    tok = P("tp", "ctx")
    return jax.shard_map(
        local,
        mesh=mesh,
        in_specs=(tok, P("tp", None), tok, tok, tok, tok, tok, P("tp")),
        out_specs=(tok, tok, tok, tok, tok, P("tp")),
        check_vma=False,
    )
```

```python
import functools

import jax
import jax.numpy as jnp
import numpy as np
from jax import lax
from jax.experimental import pallas as pl
from jax.experimental.pallas import tpu as pltpu
from jax.sharding import PartitionSpec as P


bf16 = jnp.bfloat16
f32 = jnp.float32
VM = pl.BlockSpec(memory_space=pltpu.VMEM)
HBM = pl.BlockSpec(memory_space=pltpu.HBM)


def hi_lo(table):
    high = table.astype(np.float32).astype(bf16)
    low = (table - high.astype(np.float64)).astype(np.float32).astype(bf16)
    return np.stack([high, low])


def dft_tables(blocks, per, width):
    full = 2 * blocks
    k = np.arange(full)[:, None]
    a = np.arange(blocks)[None, :]
    b = np.arange(width)
    outer = np.exp(-2j * np.pi * ((k * a) % full) / full)
    twist = np.exp(-2j * np.pi * ((k * b[None, :]) % (full * width)) / (full * width))
    inner = np.exp(-2j * np.pi * ((b[:, None] * b[None, :]) % width) / width)
    fwd = hi_lo(np.repeat(np.stack([outer.real, outer.imag]), per, axis=2))
    back = hi_lo(np.repeat(np.stack([outer.real.T, outer.imag.T]), per, axis=2))[0]
    inner = hi_lo(np.concatenate([inner.real, inner.imag], 1))[0]
    twist = np.stack([twist.real, twist.imag]).astype(np.float32)
    return jnp.asarray(fwd), jnp.asarray(back), jnp.asarray(inner), jnp.asarray(twist)


def dot(left, right):
    return jnp.dot(left, right, preferred_element_type=f32)


def spread_rows(table, per):
    n, lanes = table.shape
    wide = jnp.broadcast_to(table.astype(f32)[:, None, :], (n, per, lanes))
    row = lax.broadcasted_iota(jnp.int32, (n, per, lanes), 1)
    lane = lax.broadcasted_iota(jnp.int32, (n, per, lanes), 2) % per
    return jnp.where(row == lane, wide, 0.0).reshape(n * per, lanes).astype(bf16)


def twisted(re, im, tw_ref, per, sign):
    n, width = tw_ref.shape[1:]
    re = re.reshape(n, per, width)
    im = im.reshape(n, per, width)
    tre = tw_ref[0][:, None, :]
    tim = tw_ref[1][:, None, :] * sign
    return (re * tre - im * tim).reshape(n * per, width), (re * tim + im * tre).reshape(n * per, width)


def inner_dft(re, im, table, sign):
    width = table.shape[0]
    r = dot(re.astype(bf16), table)
    i = dot(im.astype(bf16), table)
    if sign > 0:
        return r[:, :width] - i[:, width:], r[:, width:] + i[:, :width]
    return r[:, :width] + i[:, width:], i[:, :width] - r[:, width:]


def row_scale(x, per):
    top = jnp.max(jnp.max(jnp.abs(x.astype(f32)).reshape(-1, per, x.shape[1]), axis=0), axis=1, keepdims=True)
    return jnp.where(top > 0.0, top, 1.0)[None]


def scaled(x, factor):
    per = factor.shape[1]
    return (x.reshape(-1, per, x.shape[1]) * factor).reshape(x.shape)


def spectral_kernel(msg_ref, *refs, per, blocks, width):
    sources, out_ref, (fwd_ref, back_ref, b_ref, tw_ref), sems = refs[:4], refs[4], refs[5:9], refs[9]
    copies = [pltpu.make_async_copy(src, dst, sems.at[n]) for n, (src, dst) in enumerate(zip(sources, refs[5:9]))]
    for n in (0, 3, 2, 1):
        copies[n].start()
    rows = 2 * blocks * per
    half = blocks * per
    g, p, f = [msg_ref[:, n * per : (n + 1) * per, :].reshape(half, width) for n in range(3)]
    p_top = row_scale(p, per)
    f_top = row_scale(f, per)
    copies[0].wait()
    high, low = [
        jnp.concatenate([spread_rows(fwd_ref[h, c], per) for c in range(2)], 0) for h in range(2)
    ]
    g1, p1, f1 = [dot(high, x) + dot(low, x) for x in (g, p, f)]
    p1 = scaled(p1, 1.0 / p_top)
    f1 = scaled(f1, 1.0 / f_top)
    copies[3].wait()
    copies[2].wait()
    table = b_ref[...]
    gre, gim = inner_dft(*twisted(g1[:rows], g1[rows:], tw_ref, per, 1.0), table, 1)
    zre, zim = inner_dft(*twisted(p1[:rows] + f1[rows:], p1[rows:] - f1[:rows], tw_ref, per, 1.0), table, 1)
    re, im = inner_dft(gre * zre + gim * zim, gim * zre - gre * zim, table, -1)
    re, im = twisted(re, im, tw_ref, per, -1.0)
    scale = 1.0 / (2 * blocks * width)
    re = (re * scale).astype(bf16)
    im = (im * scale).astype(bf16)
    copies[1].wait()
    mat_re, mat_im = [spread_rows(back_ref[c], per) for c in range(2)]
    lag = scaled(dot(mat_re, re) + dot(mat_im, im), p_top)
    conv = scaled(dot(mat_re, im) - dot(mat_im, re), f_top)
    out_ref[:, :per, :] = lag.astype(bf16).reshape(blocks, per, width)
    out_ref[:, per : 2 * per, :] = conv.astype(bf16).reshape(blocks, per, width)
    prod = (g.astype(f32) * p.astype(f32)).reshape(blocks, per, width)
    total = jnp.sum(jnp.sum(prod, axis=0), axis=1, keepdims=True)
    row = lax.broadcasted_iota(jnp.int32, (per, width), 0)
    lane = lax.broadcasted_iota(jnp.int32, (per, width), 1) % per
    total = jnp.sum(jnp.where(row == lane, total, 0.0), axis=0, keepdims=True)
    high = total.astype(bf16).astype(f32)
    eighth = per // 2
    which = lax.broadcasted_iota(jnp.int32, (eighth, width), 0)
    extra = jnp.where(which == 0, high, jnp.where(which == 1, total - high, 0.0)).astype(bf16)
    out_ref[:, 2 * per :, :] = jnp.broadcast_to(extra[None], (blocks, eighth, width))


def in_hbm(x):
    return pltpu.with_memory_space_constraint(x, pltpu.HBM)


def limit(mib):
    return pltpu.CompilerParams(vmem_limit_bytes=mib << 20)


def cost(flops, bytes_accessed):
    return pl.CostEstimate(flops=flops, bytes_accessed=bytes_accessed, transcendentals=0)


def spectral(msg, tables):
    blocks, triple, width = msg.shape
    per = triple // 3
    return pl.pallas_call(
        functools.partial(spectral_kernel, per=per, blocks=blocks, width=width),
        out_shape=jax.ShapeDtypeStruct((blocks, 2 * per + per // 2, width), bf16),
        in_specs=[VM] + [HBM] * 4,
        out_specs=VM,
        scratch_shapes=[pltpu.VMEM(t.shape, t.dtype) for t in tables] + [pltpu.SemaphoreType.DMA((4,))],
        name="spectral",
        compiler_params=limit(20),
        cost_estimate=cost(2 * 14000 * 256 * 256, 2 << 20),
    )(msg, *[in_hbm(t) for t in tables])


SHIFTS = (0, 1, -1, 2)


def position():
    ctx = lax.axis_index("ctx")
    tp = lax.axis_index("tp")
    return ctx >> 1, ctx & 1, tp >> 2, (tp >> 1) & 1, tp & 1


def gated_kernel(*refs, per):
    sources = refs[:7]
    blocks = list(refs[7:22])
    gate_grad_ref, msg_ref, own_out_ref, gated_ref = refs[22:26]
    buffers, sems = refs[26:33], refs[33]
    copies = [pltpu.make_async_copy(src, dst, sems.at[n]) for n, (src, dst) in enumerate(zip(sources, buffers))]
    for copy in copies:
        copy.start()
    own_ref, w_ref, gate_ref, conv_ref, key_ref, value_ref, filt_ref = buffers
    groups, _, width = msg_ref.shape
    _, _, y, xl, core = position()
    for n in (0, 2, 3, 4, 5, 6):
        copies[n].wait()
    own_out_ref[...] = own_ref[...]
    gated_ref[...] = (gate_ref[...].astype(f32) * conv_ref[...].astype(f32)).astype(bf16)
    product = (key_ref[...].astype(f32) * value_ref[...].astype(f32)).astype(bf16)
    msg_ref[:, per : 2 * per, :] = product.reshape(groups, per, width)
    msg_ref[:, 2 * per :, :] = filt_ref[...].reshape(groups, per, width)
    copies[1].wait()
    total = jnp.zeros(gate_grad_ref.shape, f32)
    for n, block in enumerate([own_ref] + blocks):
        index = (((y - SHIFTS[n % 4]) & 3) * 2 + (xl ^ (n // 4 % 2))) * 2 + (core ^ (n // 8))
        total = total + dot(w_ref[:, pl.ds(pl.multiple_of(index * width, width), width)], block[...])
    gate_grad_ref[...] = (total * conv_ref[...].astype(f32)).astype(bf16)
    msg_ref[:, :per, :] = (total * gate_ref[...].astype(f32)).astype(bf16).reshape(groups, per, width)


def gated_grads(weight, gate, conv_out, key_in, value_in, filt, blocks, groups):
    channels, width = gate.shape
    per = channels // groups
    small = pltpu.VMEM(gate.shape, bf16)
    shape = jax.ShapeDtypeStruct(gate.shape, bf16)
    held = [blocks[0], weight, gate, conv_out, key_in, value_in, filt]
    return pl.pallas_call(
        functools.partial(gated_kernel, per=per),
        out_shape=(shape, jax.ShapeDtypeStruct((groups, 3 * per, width), bf16), shape, shape),
        in_specs=[HBM] * 7 + [VM] * 15,
        out_specs=(VM,) * 4,
        scratch_shapes=[small, pltpu.VMEM(weight.shape, bf16)] + [small] * 5 + [pltpu.SemaphoreType.DMA((7,))],
        name="gated_grads",
        compiler_params=limit(6),
        cost_estimate=cost(2 * gate.size * weight.shape[1], 5 << 20),
    )(*[in_hbm(x) for x in held], *blocks[1:])


def pack_kernel(gated_ref, *refs):
    blocks = refs[:16]
    side_ref, down_ref, cross_ref, mine_ref = refs[16:]
    z, h, y, xl, core = position()
    for ref in (side_ref, down_ref, cross_ref):
        ref[2] = gated_ref[...]
    mine_ref[4] = gated_ref[...]
    keep = (core ^ h) * 2 + (xl ^ (z & 1))
    for q in range(4):

        @pl.when(keep == q)
        def _():
            for n, d in enumerate(SHIFTS):
                row = (y - d) & 3
                mine_ref[row] = blocks[q * 4 + n][...]

                @pl.when((row >> 1) == core)
                def _():
                    for ref, turn in ((side_ref, 2), (down_ref, 1), (cross_ref, 3)):
                        ref[row & 1] = blocks[(q ^ turn) * 4 + n][...]


def pack(gated, blocks):
    shape = gated.shape
    return pl.pallas_call(
        pack_kernel,
        out_shape=tuple(jax.ShapeDtypeStruct((n,) + shape, bf16) for n in (3, 3, 3, 5)),
        in_specs=[VM] * 17,
        out_specs=(VM,) * 4,
        name="pack",
        compiler_params=limit(3),
        cost_estimate=cost(gated.size, 4 << 20),
    )(gated, *blocks)


def weight_kernel(after_hbm, mine_ref, *refs):
    received = refs[:3]
    swapped = refs[3:6]
    own_ref, *outs, sum_ref = refs[6:]
    z, _, _, _, core = position()

    def outer(rows, block):
        return lax.dot_general(rows, block, (((1,), (1,)), ((), ())), preferred_element_type=f32)

    rows = [mine_ref[4]] + [ref[2] for ref in received]
    for half, source in ((core, received), (1 - core, swapped)):
        for i in range(2):
            r = 2 * half + i
            total = outer(rows[0], mine_ref[r])
            for m in range(3):
                total = total + outer(rows[m + 1], source[m][i])
            sum_ref[r] = total
    own_ref[...] = sum_ref[z >> 1]
    for out, d in zip(outs, (2, 1, 3)):
        out[...] = sum_ref[((z >> 1) + d) & 3].astype(bf16)


def weight_parts(mine, received, swapped, after):
    shape = mine.shape[1:]
    return pl.pallas_call(
        weight_kernel,
        out_shape=(jax.ShapeDtypeStruct(shape, f32),) + (jax.ShapeDtypeStruct(shape, bf16),) * 3,
        in_specs=[HBM] + [VM] * 7,
        out_specs=(VM,) * 4,
        scratch_shapes=[pltpu.VMEM((4,) + shape, f32)],
        name="weight_parts",
        compiler_params=limit(8),
        cost_estimate=cost(2 * 16 * 256**3, 4 << 20),
    )(in_hbm(after), mine, *received, *swapped)


def final_kernel(back_ref, msg_ref, key_ref, value_ref, skip_ref, filter_ref, dkey_ref, dvalue_ref, bias_ref, *, per):
    groups, _, width = back_ref.shape
    channels = groups * per
    filter_ref[...] = back_ref[:, :per, :].reshape(channels, width)
    conv = back_ref[:, per : 2 * per, :].reshape(channels, width).astype(f32)
    grad = msg_ref[:, :per, :].reshape(channels, width).astype(f32)
    total = (conv + skip_ref[...] * grad).astype(bf16).astype(f32)
    dkey_ref[...] = (total * value_ref[...].astype(f32)).astype(bf16)
    dvalue_ref[...] = (total * key_ref[...].astype(f32)).astype(bf16)
    extra = back_ref[:, 2 * per :, :].astype(f32)
    pair = extra[:, 0, :] + extra[:, 1, :]
    row = lax.broadcasted_iota(jnp.int32, (groups, width), 0)
    lane = lax.broadcasted_iota(jnp.int32, (groups, width), 1) // per
    bias_ref[...] = jnp.sum(jnp.where(row == lane, pair, 0.0), axis=0, keepdims=True)


def final(back, msg, key_in, value_in, skip_bias):
    shape = jax.ShapeDtypeStruct(key_in.shape, bf16)
    channels = key_in.shape[0]
    per = channels // back.shape[0]
    return pl.pallas_call(
        functools.partial(final_kernel, per=per),
        out_shape=(shape, shape, shape, jax.ShapeDtypeStruct((1, channels), f32)),
        in_specs=[VM] * 5,
        out_specs=(VM,) * 4,
        name="final",
        compiler_params=limit(6),
        cost_estimate=cost(8 * key_in.size, 1 << 20),
    )(back, msg, key_in, value_in, skip_bias[:, None])


def sum_kernel(after_hbm, own_ref, one_ref, two_ref, three_ref, out_ref):
    total = own_ref[...] + one_ref[...].astype(f32)
    out_ref[...] = total + (two_ref[...].astype(f32) + three_ref[...].astype(f32))


def sum_parts(own, parts, after):
    return pl.pallas_call(
        sum_kernel,
        out_shape=jax.ShapeDtypeStruct(own.shape, f32),
        in_specs=[HBM] + [VM] * 4,
        out_specs=VM,
        name="sum_parts",
        compiler_params=limit(3),
        cost_estimate=cost(4 * own.size, 1 << 20),
    )(in_hbm(after), own, *parts)


def swap(x, axis, teams=None):
    return lax.all_to_all(x, axis, split_axis=0, concat_axis=0, axis_index_groups=teams, tiled=True)


def tp_moves():
    place = [(y, x, c) for y in range(4) for x in range(2) for c in range(2)]

    def index(y, x, c):
        return ((y % 4) * 2 + x) * 2 + c

    def step(d):
        return [(index(y, x, c), index(y + d, x, c)) for y, x, c in place]

    side = [(index(y, x, c), index(y, 1 - x, c)) for y, x, c in place]
    core = [(index(y, x, c), index(y, x, 1 - c)) for y, x, c in place]
    return step, side, core


def gather_tp(x):
    step, side, core = tp_moves()
    held = [x] + [lax.ppermute(x, "tp", step(d)) for d in SHIFTS[1:]]
    held = held + [lax.ppermute(b, "tp", side) for b in held]
    return held + [lax.ppermute(b, "tp", core) for b in held]


def ctx_moves():
    place = [(z, h) for z in range(8) for h in range(2)]
    side = [(z * 2 + h, z * 2 + 1 - h) for z, h in place]
    down = [(z * 2 + h, ((z - 1) % 8) * 2 + h) for z, h in place]
    cross = [(z * 2 + h, ((z + 1) % 8) * 2 + 1 - h) for z, h in place]
    teams = [[(2 * r + odd) * 2 + h for r in range(4)] for odd in range(2) for h in range(2)]
    return (side, down, cross), teams


def local(grad_out, out_weight, gate, key_in, value_in, conv_out, filt, skip_bias):
    channels, toks = gate.shape
    groups = lax.axis_size("ctx")
    per = channels // groups
    blocks = gather_tp(grad_out)
    near, _ = ctx_moves()
    gate_grad, msg, own_block, gated = gated_grads(
        out_weight, gate, conv_out, key_in, value_in, filt, blocks, groups
    )
    whole = swap(msg, "ctx")
    *messages, mine = pack(gated, [own_block] + blocks[1:])
    received = []
    for message, move in zip(messages, near):
        received.append(lax.ppermute(message, "ctx", move))
    core = tp_moves()[2]
    swapped = []
    for r in received:
        swapped.append(lax.ppermute(r, "tp", core))
    result = spectral(whole, dft_tables(groups, per, toks))
    back = swap(result, "ctx")
    own, *parts = weight_parts(mine, received, swapped, result)
    parts = [
        lax.ppermute(part, "ctx", [(z * 2 + h, ((z + 2 * d) % 8) * 2 + h) for z in range(8) for h in range(2)])
        for part, d in zip(parts, (2, 1, 3))
    ]
    filter_grad, key_grad, value_grad, bias_grad = final(back, msg, key_in, value_in, skip_bias)
    weight_grad = sum_parts(own, parts, filter_grad)
    return (gate_grad, key_grad, value_grad, filter_grad, weight_grad, bias_grad.reshape(channels))


def solution(mesh):
    tok = P("tp", "ctx")
    return jax.shard_map(
        local,
        mesh=mesh,
        in_specs=(tok, P("tp", None), tok, tok, tok, tok, tok, P("tp")),
        out_specs=(tok, tok, tok, tok, tok, P("tp")),
        check_vma=False,
    )
```

```python
import functools

import jax
import jax.numpy as jnp
import numpy as np
from jax import lax
from jax.experimental import pallas as pl
from jax.experimental.pallas import tpu as pltpu
from jax.sharding import PartitionSpec as P


bf16 = jnp.bfloat16
f32 = jnp.float32
VM = pl.BlockSpec(memory_space=pltpu.VMEM)
HBM = pl.BlockSpec(memory_space=pltpu.HBM)


def hi_lo(table):
    high = table.astype(np.float32).astype(bf16)
    low = (table - high.astype(np.float64)).astype(np.float32).astype(bf16)
    return np.stack([high, low])


def dft_tables(blocks, per, width):
    full = 2 * blocks
    k = np.arange(full)[:, None]
    a = np.arange(blocks)[None, :]
    b = np.arange(width)
    outer = np.exp(-2j * np.pi * ((k * a) % full) / full)
    twist = np.exp(-2j * np.pi * ((k * b[None, :]) % (full * width)) / (full * width))
    inner = np.exp(-2j * np.pi * ((b[:, None] * b[None, :]) % width) / width)
    fwd = hi_lo(np.repeat(np.stack([outer.real, outer.imag]), per, axis=2))
    back = hi_lo(np.repeat(np.stack([outer.real.T, outer.imag.T]), per, axis=2))[0]
    inner = hi_lo(np.concatenate([inner.real, inner.imag], 1))[0]
    twist = np.stack([twist.real, twist.imag]).astype(np.float32)
    return jnp.asarray(fwd), jnp.asarray(back), jnp.asarray(inner), jnp.asarray(twist)


def dot(left, right):
    return jnp.dot(left, right, preferred_element_type=f32)


def spread_rows(table, per):
    n, lanes = table.shape
    wide = jnp.broadcast_to(table.astype(f32)[:, None, :], (n, per, lanes))
    row = lax.broadcasted_iota(jnp.int32, (n, per, lanes), 1)
    lane = lax.broadcasted_iota(jnp.int32, (n, per, lanes), 2) % per
    return jnp.where(row == lane, wide, 0.0).reshape(n * per, lanes).astype(bf16)


def twisted(re, im, tw_ref, per, sign):
    n, width = tw_ref.shape[1:]
    re = re.reshape(n, per, width)
    im = im.reshape(n, per, width)
    tre = tw_ref[0][:, None, :]
    tim = tw_ref[1][:, None, :] * sign
    return (re * tre - im * tim).reshape(n * per, width), (re * tim + im * tre).reshape(n * per, width)


def inner_dft(re, im, table, sign):
    width = table.shape[0]
    r = dot(re.astype(bf16), table)
    i = dot(im.astype(bf16), table)
    if sign > 0:
        return r[:, :width] - i[:, width:], r[:, width:] + i[:, :width]
    return r[:, :width] + i[:, width:], i[:, :width] - r[:, width:]


def row_scale(x, per):
    wide = x.astype(f32).reshape(-1, per, x.shape[1])
    top = jnp.max(jnp.max(jnp.abs(wide), axis=0), axis=1, keepdims=True)
    top = jnp.where(top > 0.0, top, 1.0)
    wide = wide * (1.0 / top)[None]
    square = jnp.sum(jnp.sum(wide * wide, axis=0), axis=1, keepdims=True)
    root = top * jnp.sqrt(square * (1.0 / (wide.shape[0] * wide.shape[2])))
    return jnp.where(root > 0.0, root, 1.0)[None]


def scaled(x, factor):
    per = factor.shape[1]
    return (x.reshape(-1, per, x.shape[1]) * factor).reshape(x.shape)


def spectral_kernel(msg_ref, *refs, per, blocks, width):
    sources, out_ref, (fwd_ref, back_ref, b_ref, tw_ref), sems = refs[:4], refs[4], refs[5:9], refs[9]
    copies = [pltpu.make_async_copy(src, dst, sems.at[n]) for n, (src, dst) in enumerate(zip(sources, refs[5:9]))]
    for n in (0, 3, 2, 1):
        copies[n].start()
    rows = 2 * blocks * per
    half = blocks * per
    g, p, f = [msg_ref[:, n * per : (n + 1) * per, :].reshape(half, width) for n in range(3)]
    p_top = row_scale(p, per)
    f_top = row_scale(f, per)
    copies[0].wait()
    high, low = [
        jnp.concatenate([spread_rows(fwd_ref[h, c], per) for c in range(2)], 0) for h in range(2)
    ]
    g1, p1, f1 = [dot(high, x) + dot(low, x) for x in (g, p, f)]
    p1 = scaled(p1, 1.0 / p_top)
    f1 = scaled(f1, 1.0 / f_top)
    copies[3].wait()
    copies[2].wait()
    table = b_ref[...]
    gre, gim = inner_dft(*twisted(g1[:rows], g1[rows:], tw_ref, per, 1.0), table, 1)
    zre, zim = inner_dft(*twisted(p1[:rows] + f1[rows:], p1[rows:] - f1[:rows], tw_ref, per, 1.0), table, 1)
    re, im = inner_dft(gre * zre + gim * zim, gim * zre - gre * zim, table, -1)
    re, im = twisted(re, im, tw_ref, per, -1.0)
    scale = 1.0 / (2 * blocks * width)
    re = (re * scale).astype(bf16)
    im = (im * scale).astype(bf16)
    copies[1].wait()
    mat_re, mat_im = [spread_rows(back_ref[c], per) for c in range(2)]
    lag = scaled(dot(mat_re, re) + dot(mat_im, im), p_top)
    conv = scaled(dot(mat_re, im) - dot(mat_im, re), f_top)
    cut = width // 2
    for n, x in enumerate((lag, conv)):
        for side in range(2):
            rows_at = (2 * n + side) * per
            piece = x[:, side * cut : (side + 1) * cut].astype(bf16).reshape(blocks, per, cut)
            out_ref[:, rows_at : rows_at + per, :] = piece
    prod = (g.astype(f32) * p.astype(f32)).reshape(blocks, per, width)
    total = jnp.sum(jnp.sum(prod, axis=0), axis=1, keepdims=True)
    row = lax.broadcasted_iota(jnp.int32, (per, cut), 0)
    lane = lax.broadcasted_iota(jnp.int32, (per, cut), 1) % per
    total = jnp.sum(jnp.where(row == lane, total, 0.0), axis=0, keepdims=True)
    high = total.astype(bf16).astype(f32)
    eighth = per // 2
    which = lax.broadcasted_iota(jnp.int32, (eighth, cut), 0)
    extra = jnp.where(which == 0, high, jnp.where(which == 1, total - high, 0.0)).astype(bf16)
    out_ref[:, 4 * per :, :] = jnp.broadcast_to(extra[None], (blocks, eighth, cut))


def in_hbm(x):
    return pltpu.with_memory_space_constraint(x, pltpu.HBM)


def limit(mib):
    return pltpu.CompilerParams(vmem_limit_bytes=mib << 20)


def cost(flops, bytes_accessed):
    return pl.CostEstimate(flops=flops, bytes_accessed=bytes_accessed, transcendentals=0)


def spectral(msg, tables):
    blocks, triple, width = msg.shape
    per = triple // 3
    return pl.pallas_call(
        functools.partial(spectral_kernel, per=per, blocks=blocks, width=width),
        out_shape=jax.ShapeDtypeStruct((blocks, 4 * per + per // 2, width // 2), bf16),
        in_specs=[VM] + [HBM] * 4,
        out_specs=VM,
        scratch_shapes=[pltpu.VMEM(t.shape, t.dtype) for t in tables] + [pltpu.SemaphoreType.DMA((4,))],
        name="spectral",
        compiler_params=limit(20),
        cost_estimate=cost(2 * 14000 * 256 * 256, 2 << 20),
    )(msg, *[in_hbm(t) for t in tables])


SHIFTS = (0, 1, -1, 2)


def position():
    ctx = lax.axis_index("ctx")
    tp = lax.axis_index("tp")
    return ctx >> 1, ctx & 1, tp >> 2, (tp >> 1) & 1, tp & 1


def gated_kernel(*refs, per):
    sources = refs[:7]
    blocks = list(refs[7:22])
    gate_grad_ref, msg_ref, own_out_ref, gated_ref = refs[22:26]
    buffers, sems = refs[26:33], refs[33]
    copies = [pltpu.make_async_copy(src, dst, sems.at[n]) for n, (src, dst) in enumerate(zip(sources, buffers))]
    for copy in copies:
        copy.start()
    own_ref, w_ref, gate_ref, conv_ref, key_ref, value_ref, filt_ref = buffers
    groups, _, width = msg_ref.shape
    _, _, y, xl, core = position()
    for n in (0, 2, 3, 4, 5, 6):
        copies[n].wait()
    own_out_ref[...] = own_ref[...]
    gated_ref[...] = (gate_ref[...].astype(f32) * conv_ref[...].astype(f32)).astype(bf16)
    product = (key_ref[...].astype(f32) * value_ref[...].astype(f32)).astype(bf16)
    msg_ref[:, per : 2 * per, :] = product.reshape(groups, per, width)
    msg_ref[:, 2 * per :, :] = filt_ref[...].reshape(groups, per, width)
    copies[1].wait()
    total = jnp.zeros(gate_grad_ref.shape, f32)
    for n, block in enumerate([own_ref] + blocks):
        index = (((y - SHIFTS[n % 4]) & 3) * 2 + (xl ^ (n // 4 % 2))) * 2 + (core ^ (n // 8))
        total = total + dot(w_ref[:, pl.ds(pl.multiple_of(index * width, width), width)], block[...])
    gate_grad_ref[...] = (total * conv_ref[...].astype(f32)).astype(bf16)
    msg_ref[:, :per, :] = (total * gate_ref[...].astype(f32)).astype(bf16).reshape(groups, per, width)


def gated_grads(weight, gate, conv_out, key_in, value_in, filt, blocks, groups):
    channels, width = gate.shape
    per = channels // groups
    small = pltpu.VMEM(gate.shape, bf16)
    shape = jax.ShapeDtypeStruct(gate.shape, bf16)
    held = [blocks[0], weight, gate, conv_out, key_in, value_in, filt]
    return pl.pallas_call(
        functools.partial(gated_kernel, per=per),
        out_shape=(shape, jax.ShapeDtypeStruct((groups, 3 * per, width), bf16), shape, shape),
        in_specs=[HBM] * 7 + [VM] * 15,
        out_specs=(VM,) * 4,
        scratch_shapes=[small, pltpu.VMEM(weight.shape, bf16)] + [small] * 5 + [pltpu.SemaphoreType.DMA((7,))],
        name="gated_grads",
        compiler_params=limit(6),
        cost_estimate=cost(2 * gate.size * weight.shape[1], 5 << 20),
    )(*[in_hbm(x) for x in held], *blocks[1:])


def pack_kernel(gated_ref, *refs):
    blocks = refs[:16]
    side_ref, down_ref, cross_ref, mine_ref = refs[16:]
    z, h, y, xl, core = position()
    for ref in (side_ref, down_ref, cross_ref):
        ref[2] = gated_ref[...]
    mine_ref[4] = gated_ref[...]
    keep = (core ^ h) * 2 + (xl ^ (z & 1))
    for q in range(4):

        @pl.when(keep == q)
        def _():
            for n, d in enumerate(SHIFTS):
                row = (y - d) & 3
                mine_ref[row] = blocks[q * 4 + n][...]

                @pl.when((row >> 1) == core)
                def _():
                    for ref, turn in ((side_ref, 2), (down_ref, 1), (cross_ref, 3)):
                        ref[row & 1] = blocks[(q ^ turn) * 4 + n][...]


def pack(gated, blocks):
    shape = gated.shape
    return pl.pallas_call(
        pack_kernel,
        out_shape=tuple(jax.ShapeDtypeStruct((n,) + shape, bf16) for n in (3, 3, 3, 5)),
        in_specs=[VM] * 17,
        out_specs=(VM,) * 4,
        name="pack",
        compiler_params=limit(3),
        cost_estimate=cost(gated.size, 4 << 20),
    )(gated, *blocks)


def weight_kernel(after_hbm, mine_ref, *refs):
    received = refs[:3]
    swapped = refs[3:6]
    own_ref, *outs, sum_ref = refs[6:]
    z, _, _, _, core = position()

    def outer(rows, block):
        return lax.dot_general(rows, block, (((1,), (1,)), ((), ())), preferred_element_type=f32)

    rows = [mine_ref[4]] + [ref[2] for ref in received]
    for half, source in ((core, received), (1 - core, swapped)):
        for i in range(2):
            r = 2 * half + i
            total = outer(rows[0], mine_ref[r])
            for m in range(3):
                total = total + outer(rows[m + 1], source[m][i])
            sum_ref[r] = total
    own_ref[...] = sum_ref[z >> 1]
    for out, d in zip(outs, (2, 1, 3)):
        out[...] = sum_ref[((z >> 1) + d) & 3].astype(bf16)


def weight_parts(mine, received, swapped, after):
    shape = mine.shape[1:]
    return pl.pallas_call(
        weight_kernel,
        out_shape=(jax.ShapeDtypeStruct(shape, f32),) + (jax.ShapeDtypeStruct(shape, bf16),) * 3,
        in_specs=[HBM] + [VM] * 7,
        out_specs=(VM,) * 4,
        scratch_shapes=[pltpu.VMEM((4,) + shape, f32)],
        name="weight_parts",
        compiler_params=limit(8),
        cost_estimate=cost(2 * 16 * 256**3, 4 << 20),
    )(in_hbm(after), mine, *received, *swapped)


def final_kernel(back_ref, msg_ref, key_ref, value_ref, skip_ref, filter_ref, dkey_ref, dvalue_ref, bias_ref, *, per):
    groups, _, cut = back_ref.shape
    channels = groups * per

    def whole(n):
        pieces = [back_ref[:, (2 * n + side) * per : (2 * n + side + 1) * per, :] for side in range(2)]
        return jnp.concatenate([piece.reshape(channels, cut) for piece in pieces], 1)

    filter_ref[...] = whole(0)
    conv = whole(1).astype(f32)
    grad = msg_ref[:, :per, :].reshape(channels, 2 * cut).astype(f32)
    total = (conv + skip_ref[...] * grad).astype(bf16).astype(f32)
    dkey_ref[...] = (total * value_ref[...].astype(f32)).astype(bf16)
    dvalue_ref[...] = (total * key_ref[...].astype(f32)).astype(bf16)
    extra = back_ref[:, 4 * per :, :].astype(f32)
    pair = extra[:, 0, :] + extra[:, 1, :]
    pair = jnp.concatenate([pair] * (channels // cut), 1)
    row = lax.broadcasted_iota(jnp.int32, (groups, channels), 0)
    lane = lax.broadcasted_iota(jnp.int32, (groups, channels), 1) // per
    bias_ref[...] = jnp.sum(jnp.where(row == lane, pair, 0.0), axis=0, keepdims=True)


def final(back, msg, key_in, value_in, skip_bias):
    shape = jax.ShapeDtypeStruct(key_in.shape, bf16)
    channels = key_in.shape[0]
    per = channels // back.shape[0]
    return pl.pallas_call(
        functools.partial(final_kernel, per=per),
        out_shape=(shape, shape, shape, jax.ShapeDtypeStruct((1, channels), f32)),
        in_specs=[VM] * 5,
        out_specs=(VM,) * 4,
        name="final",
        compiler_params=limit(6),
        cost_estimate=cost(8 * key_in.size, 1 << 20),
    )(back, msg, key_in, value_in, skip_bias[:, None])


def sum_kernel(after_hbm, own_ref, one_ref, two_ref, three_ref, out_ref):
    total = own_ref[...] + one_ref[...].astype(f32)
    out_ref[...] = total + (two_ref[...].astype(f32) + three_ref[...].astype(f32))


def sum_parts(own, parts, after):
    return pl.pallas_call(
        sum_kernel,
        out_shape=jax.ShapeDtypeStruct(own.shape, f32),
        in_specs=[HBM] + [VM] * 4,
        out_specs=VM,
        name="sum_parts",
        compiler_params=limit(3),
        cost_estimate=cost(4 * own.size, 1 << 20),
    )(in_hbm(after), own, *parts)


def swap(x, axis, teams=None):
    return lax.all_to_all(x, axis, split_axis=0, concat_axis=0, axis_index_groups=teams, tiled=True)


def tp_moves():
    place = [(y, x, c) for y in range(4) for x in range(2) for c in range(2)]

    def index(y, x, c):
        return ((y % 4) * 2 + x) * 2 + c

    def step(d):
        return [(index(y, x, c), index(y + d, x, c)) for y, x, c in place]

    side = [(index(y, x, c), index(y, 1 - x, c)) for y, x, c in place]
    core = [(index(y, x, c), index(y, x, 1 - c)) for y, x, c in place]
    return step, side, core


def gather_tp(x):
    step, side, core = tp_moves()
    across = lax.ppermute(x, "tp", side)
    near = []
    for d in SHIFTS[1:]:
        near.append(lax.ppermute(x, "tp", step(d)))
    far = [lax.ppermute(b, "tp", side) for b in near[:2]] + [lax.ppermute(across, "tp", step(2))]
    held = [x] + near + [across] + far
    return held + [lax.ppermute(b, "tp", core) for b in held]


def ctx_moves():
    place = [(z, h) for z in range(8) for h in range(2)]
    side = [(z * 2 + h, z * 2 + 1 - h) for z, h in place]
    down = [(z * 2 + h, ((z - 1) % 8) * 2 + h) for z, h in place]
    cross = [(z * 2 + h, ((z + 1) % 8) * 2 + 1 - h) for z, h in place]
    teams = [[(2 * r + odd) * 2 + h for r in range(4)] for odd in range(2) for h in range(2)]
    return (side, down, cross), teams


def local(grad_out, out_weight, gate, key_in, value_in, conv_out, filt, skip_bias):
    channels, toks = gate.shape
    groups = lax.axis_size("ctx")
    per = channels // groups
    blocks = gather_tp(grad_out)
    near, _ = ctx_moves()
    gate_grad, msg, own_block, gated = gated_grads(
        out_weight, gate, conv_out, key_in, value_in, filt, blocks, groups
    )
    whole = swap(msg, "ctx")
    *messages, mine = pack(gated, [own_block] + blocks[1:])
    received = []
    for message, move in zip(messages, near):
        received.append(lax.ppermute(message, "ctx", move))
    core = tp_moves()[2]
    swapped = []
    for r in received:
        swapped.append(lax.ppermute(r, "tp", core))
    result = spectral(whole, dft_tables(groups, per, toks))
    back = swap(result, "ctx")
    own, *parts = weight_parts(mine, received, swapped, result)
    parts = [
        lax.ppermute(part, "ctx", [(z * 2 + h, ((z + 2 * d) % 8) * 2 + h) for z in range(8) for h in range(2)])
        for part, d in zip(parts, (2, 1, 3))
    ]
    filter_grad, key_grad, value_grad, bias_grad = final(back, msg, key_in, value_in, skip_bias)
    weight_grad = sum_parts(own, parts, filter_grad)
    return (gate_grad, key_grad, value_grad, filter_grad, weight_grad, bias_grad.reshape(channels))


def solution(mesh):
    tok = P("tp", "ctx")
    return jax.shard_map(
        local,
        mesh=mesh,
        in_specs=(tok, P("tp", None), tok, tok, tok, tok, tok, P("tp")),
        out_specs=(tok, tok, tok, tok, tok, P("tp")),
        check_vma=False,
    )
```

```python
import functools

import jax
import jax.numpy as jnp
import numpy as np
from jax import lax
from jax.experimental import pallas as pl
from jax.experimental.pallas import tpu as pltpu
from jax.sharding import PartitionSpec as P


bf16 = jnp.bfloat16
f32 = jnp.float32
VM = pl.BlockSpec(memory_space=pltpu.VMEM)
HBM = pl.BlockSpec(memory_space=pltpu.HBM)


def narrow(table):
    return jnp.asarray(table.astype(np.float32).astype(bf16))


def dft_tables(blocks, per, width):
    full = 2 * blocks
    k = np.arange(full)[:, None]
    a = np.arange(blocks)[None, :]
    b = np.arange(width)
    outer = np.exp(-2j * np.pi * ((k * a) % full) / full)
    twist = np.exp(-2j * np.pi * ((k * b[None, :]) % (full * width)) / (full * width))
    inner = np.exp(-2j * np.pi * ((b[:, None] * b[None, :]) % width) / width)
    fwd = narrow(np.repeat(np.stack([outer.real, outer.imag]), per, axis=2))
    back = narrow(np.repeat(np.stack([outer.real.T, outer.imag.T]), per, axis=2))
    inner = narrow(np.concatenate([inner.real, inner.imag], 1))
    return fwd, back, inner, jnp.asarray(np.stack([twist.real, twist.imag]).astype(np.float32))


def dot(left, right):
    return jnp.dot(left, right, preferred_element_type=f32)


def spread_rows(table, per):
    n, lanes = table.shape
    wide = jnp.broadcast_to(table.astype(f32)[:, None, :], (n, per, lanes))
    row = lax.broadcasted_iota(jnp.int32, (n, per, lanes), 1)
    lane = lax.broadcasted_iota(jnp.int32, (n, per, lanes), 2) % per
    return jnp.where(row == lane, wide, 0.0).reshape(n * per, lanes).astype(bf16)


def twisted(re, im, tw_ref, per, sign):
    n, width = tw_ref.shape[1:]
    re = re.reshape(n, per, width)
    im = im.reshape(n, per, width)
    tre = tw_ref[0][:, None, :]
    tim = tw_ref[1][:, None, :] * sign
    return (re * tre - im * tim).reshape(n * per, width), (re * tim + im * tre).reshape(n * per, width)


def inner_dft(re, im, table, sign):
    width = table.shape[0]
    r = dot(re.astype(bf16), table)
    i = dot(im.astype(bf16), table)
    if sign > 0:
        return r[:, :width] - i[:, width:], r[:, width:] + i[:, :width]
    return r[:, :width] + i[:, width:], i[:, :width] - r[:, width:]


def row_scale(x, per):
    wide = x.astype(f32).reshape(-1, per, x.shape[1])
    top = jnp.max(jnp.max(jnp.abs(wide), axis=0), axis=1, keepdims=True)
    top = jnp.where(top > 0.0, top, 1.0)
    wide = wide * (1.0 / top)[None]
    square = jnp.sum(jnp.sum(wide * wide, axis=0), axis=1, keepdims=True)
    root = top * jnp.sqrt(square * (1.0 / (wide.shape[0] * wide.shape[2])))
    return jnp.where(root > 0.0, root, 1.0)[None]


def scaled(x, factor):
    per = factor.shape[1]
    return (x.reshape(-1, per, x.shape[1]) * factor).reshape(x.shape)


def spectral_kernel(msg_ref, *refs, per, blocks, width):
    sources, out_ref, (fwd_ref, back_ref, b_ref, tw_ref), sems = refs[:4], refs[4], refs[5:9], refs[9]
    copies = [pltpu.make_async_copy(src, dst, sems.at[n]) for n, (src, dst) in enumerate(zip(sources, refs[5:9]))]
    for n in (0, 3, 2, 1):
        copies[n].start()
    rows = 2 * blocks * per
    half = blocks * per
    g, p, f = [msg_ref[:, n * per : (n + 1) * per, :].reshape(half, width) for n in range(3)]
    p_top = row_scale(p, per)
    f_top = row_scale(f, per)
    copies[0].wait()
    outer = jnp.concatenate([spread_rows(fwd_ref[c], per) for c in range(2)], 0)
    g1, p1, f1 = [dot(outer, x) for x in (g, p, f)]
    p1 = scaled(p1, 1.0 / p_top)
    f1 = scaled(f1, 1.0 / f_top)
    copies[3].wait()
    copies[2].wait()
    table = b_ref[...]
    gre, gim = inner_dft(*twisted(g1[:rows], g1[rows:], tw_ref, per, 1.0), table, 1)
    zre, zim = inner_dft(*twisted(p1[:rows] + f1[rows:], p1[rows:] - f1[:rows], tw_ref, per, 1.0), table, 1)
    re, im = inner_dft(gre * zre + gim * zim, gim * zre - gre * zim, table, -1)
    re, im = twisted(re, im, tw_ref, per, -1.0)
    scale = 1.0 / (2 * blocks * width)
    re = (re * scale).astype(bf16)
    im = (im * scale).astype(bf16)
    copies[1].wait()
    mat_re, mat_im = [spread_rows(back_ref[c], per) for c in range(2)]
    lag = scaled(dot(mat_re, re) + dot(mat_im, im), p_top)
    conv = scaled(dot(mat_re, im) - dot(mat_im, re), f_top)
    cut = width // 2
    for n, x in enumerate((lag, conv)):
        for side in range(2):
            rows_at = (2 * n + side) * per
            piece = x[:, side * cut : (side + 1) * cut].astype(bf16).reshape(blocks, per, cut)
            out_ref[:, rows_at : rows_at + per, :] = piece
    prod = (g.astype(f32) * p.astype(f32)).reshape(blocks, per, width)
    total = jnp.sum(jnp.sum(prod, axis=0), axis=1, keepdims=True)
    row = lax.broadcasted_iota(jnp.int32, (per, cut), 0)
    lane = lax.broadcasted_iota(jnp.int32, (per, cut), 1) % per
    total = jnp.sum(jnp.where(row == lane, total, 0.0), axis=0, keepdims=True)
    high = total.astype(bf16).astype(f32)
    eighth = per // 2
    which = lax.broadcasted_iota(jnp.int32, (eighth, cut), 0)
    extra = jnp.where(which == 0, high, jnp.where(which == 1, total - high, 0.0)).astype(bf16)
    out_ref[:, 4 * per :, :] = jnp.broadcast_to(extra[None], (blocks, eighth, cut))


def in_hbm(x):
    return pltpu.with_memory_space_constraint(x, pltpu.HBM)


def limit(mib):
    return pltpu.CompilerParams(vmem_limit_bytes=mib << 20)


def cost(flops, bytes_accessed):
    return pl.CostEstimate(flops=flops, bytes_accessed=bytes_accessed, transcendentals=0)


def spectral(msg, tables):
    blocks, triple, width = msg.shape
    per = triple // 3
    return pl.pallas_call(
        functools.partial(spectral_kernel, per=per, blocks=blocks, width=width),
        out_shape=jax.ShapeDtypeStruct((blocks, 4 * per + per // 2, width // 2), bf16),
        in_specs=[VM] + [HBM] * 4,
        out_specs=VM,
        scratch_shapes=[pltpu.VMEM(t.shape, t.dtype) for t in tables] + [pltpu.SemaphoreType.DMA((4,))],
        name="spectral",
        compiler_params=limit(20),
        cost_estimate=cost(2 * 14000 * 256 * 256, 2 << 20),
    )(msg, *[in_hbm(t) for t in tables])


SHIFTS = (0, 1, -1, 2)


def position():
    ctx = lax.axis_index("ctx")
    tp = lax.axis_index("tp")
    return ctx >> 1, ctx & 1, tp >> 2, (tp >> 1) & 1, tp & 1


def gated_kernel(*refs, per):
    sources = refs[:7]
    blocks = list(refs[7:22])
    gate_grad_ref, msg_ref, own_out_ref, gated_ref = refs[22:26]
    buffers, sems = refs[26:33], refs[33]
    copies = [pltpu.make_async_copy(src, dst, sems.at[n]) for n, (src, dst) in enumerate(zip(sources, buffers))]
    for n in (1, 0, 2, 3, 4, 5, 6):
        copies[n].start()
    own_ref, w_ref, gate_ref, conv_ref, key_ref, value_ref, filt_ref = buffers
    groups, _, width = msg_ref.shape
    _, _, y, xl, core = position()
    for n in (0, 2, 3, 4, 5, 6):
        copies[n].wait()
    own_out_ref[...] = own_ref[...]
    gated_ref[...] = (gate_ref[...].astype(f32) * conv_ref[...].astype(f32)).astype(bf16)
    product = (key_ref[...].astype(f32) * value_ref[...].astype(f32)).astype(bf16)
    msg_ref[:, per : 2 * per, :] = product.reshape(groups, per, width)
    msg_ref[:, 2 * per :, :] = filt_ref[...].reshape(groups, per, width)
    copies[1].wait()
    total = jnp.zeros(gate_grad_ref.shape, f32)
    for n, block in enumerate([own_ref] + blocks):
        index = (((y - SHIFTS[n % 4]) & 3) * 2 + (xl ^ (n // 4 % 2))) * 2 + (core ^ (n // 8))
        total = total + dot(w_ref[:, pl.ds(pl.multiple_of(index * width, width), width)], block[...])
    gate_grad_ref[...] = (total * conv_ref[...].astype(f32)).astype(bf16)
    msg_ref[:, :per, :] = (total * gate_ref[...].astype(f32)).astype(bf16).reshape(groups, per, width)


def gated_grads(weight, gate, conv_out, key_in, value_in, filt, blocks, groups):
    channels, width = gate.shape
    per = channels // groups
    small = pltpu.VMEM(gate.shape, bf16)
    shape = jax.ShapeDtypeStruct(gate.shape, bf16)
    held = [blocks[0], weight, gate, conv_out, key_in, value_in, filt]
    return pl.pallas_call(
        functools.partial(gated_kernel, per=per),
        out_shape=(shape, jax.ShapeDtypeStruct((groups, 3 * per, width), bf16), shape, shape),
        in_specs=[HBM] * 7 + [VM] * 15,
        out_specs=(VM,) * 4,
        scratch_shapes=[small, pltpu.VMEM(weight.shape, bf16)] + [small] * 5 + [pltpu.SemaphoreType.DMA((7,))],
        name="gated_grads",
        compiler_params=limit(6),
        cost_estimate=cost(2 * gate.size * weight.shape[1], 5 << 20),
    )(*[in_hbm(x) for x in held], *blocks[1:])


def pack_kernel(gated_ref, *refs):
    blocks = refs[:16]
    side_ref, down_ref, cross_ref, mine_ref = refs[16:]
    z, h, y, xl, core = position()
    for ref in (side_ref, down_ref, cross_ref):
        ref[2] = gated_ref[...]
    mine_ref[4] = gated_ref[...]
    keep = (core ^ h) * 2 + (xl ^ (z & 1))
    for q in range(4):

        @pl.when(keep == q)
        def _():
            for n, d in enumerate(SHIFTS):
                row = (y - d) & 3
                mine_ref[row] = blocks[q * 4 + n][...]

                @pl.when((row >> 1) == core)
                def _():
                    for ref, turn in ((side_ref, 2), (down_ref, 1), (cross_ref, 3)):
                        ref[row & 1] = blocks[(q ^ turn) * 4 + n][...]


def pack(gated, blocks):
    shape = gated.shape
    return pl.pallas_call(
        pack_kernel,
        out_shape=tuple(jax.ShapeDtypeStruct((n,) + shape, bf16) for n in (3, 3, 3, 5)),
        in_specs=[VM] * 17,
        out_specs=(VM,) * 4,
        name="pack",
        compiler_params=limit(3),
        cost_estimate=cost(gated.size, 4 << 20),
    )(gated, *blocks)


def weight_kernel(after_hbm, mine_ref, *refs):
    received = refs[:3]
    swapped = refs[3:6]
    own_ref, *outs, sum_ref = refs[6:]
    z, _, _, _, core = position()

    def outer(rows, block):
        return lax.dot_general(rows, block, (((1,), (1,)), ((), ())), preferred_element_type=f32)

    rows = [mine_ref[4]] + [ref[2] for ref in received]
    for half, source in ((core, received), (1 - core, swapped)):
        for i in range(2):
            r = 2 * half + i
            total = outer(rows[0], mine_ref[r])
            for m in range(3):
                total = total + outer(rows[m + 1], source[m][i])
            sum_ref[r] = total
    own_ref[...] = sum_ref[z >> 1]
    for out, d in zip(outs, (2, 1, 3)):
        out[...] = sum_ref[((z >> 1) + d) & 3].astype(bf16)


def weight_parts(mine, received, swapped, after):
    shape = mine.shape[1:]
    return pl.pallas_call(
        weight_kernel,
        out_shape=(jax.ShapeDtypeStruct(shape, f32),) + (jax.ShapeDtypeStruct(shape, bf16),) * 3,
        in_specs=[HBM] + [VM] * 7,
        out_specs=(VM,) * 4,
        scratch_shapes=[pltpu.VMEM((4,) + shape, f32)],
        name="weight_parts",
        compiler_params=limit(8),
        cost_estimate=cost(2 * 16 * 256**3, 4 << 20),
    )(in_hbm(after), mine, *received, *swapped)


def final_kernel(back_ref, msg_ref, key_ref, value_ref, skip_ref, filter_ref, dkey_ref, dvalue_ref, bias_ref, *, per):
    groups, _, cut = back_ref.shape
    channels = groups * per

    def whole(n):
        pieces = [back_ref[:, (2 * n + side) * per : (2 * n + side + 1) * per, :] for side in range(2)]
        return jnp.concatenate([piece.reshape(channels, cut) for piece in pieces], 1)

    filter_ref[...] = whole(0)
    conv = whole(1).astype(f32)
    grad = msg_ref[:, :per, :].reshape(channels, 2 * cut).astype(f32)
    total = (conv + skip_ref[...] * grad).astype(bf16).astype(f32)
    dkey_ref[...] = (total * value_ref[...].astype(f32)).astype(bf16)
    dvalue_ref[...] = (total * key_ref[...].astype(f32)).astype(bf16)
    extra = back_ref[:, 4 * per :, :].astype(f32)
    pair = extra[:, 0, :] + extra[:, 1, :]
    pair = jnp.concatenate([pair] * (channels // cut), 1)
    row = lax.broadcasted_iota(jnp.int32, (groups, channels), 0)
    lane = lax.broadcasted_iota(jnp.int32, (groups, channels), 1) // per
    bias_ref[...] = jnp.sum(jnp.where(row == lane, pair, 0.0), axis=0, keepdims=True)


def final(back, msg, key_in, value_in, skip_bias):
    shape = jax.ShapeDtypeStruct(key_in.shape, bf16)
    channels = key_in.shape[0]
    per = channels // back.shape[0]
    return pl.pallas_call(
        functools.partial(final_kernel, per=per),
        out_shape=(shape, shape, shape, jax.ShapeDtypeStruct((1, channels), f32)),
        in_specs=[VM] * 5,
        out_specs=(VM,) * 4,
        name="final",
        compiler_params=limit(6),
        cost_estimate=cost(8 * key_in.size, 1 << 20),
    )(back, msg, key_in, value_in, skip_bias[:, None])


def sum_kernel(after_hbm, own_ref, one_ref, two_ref, three_ref, out_ref):
    total = own_ref[...] + one_ref[...].astype(f32)
    out_ref[...] = total + (two_ref[...].astype(f32) + three_ref[...].astype(f32))


def sum_parts(own, parts, after):
    return pl.pallas_call(
        sum_kernel,
        out_shape=jax.ShapeDtypeStruct(own.shape, f32),
        in_specs=[HBM] + [VM] * 4,
        out_specs=VM,
        name="sum_parts",
        compiler_params=limit(3),
        cost_estimate=cost(4 * own.size, 1 << 20),
    )(in_hbm(after), own, *parts)


def swap(x, axis, teams=None):
    return lax.all_to_all(x, axis, split_axis=0, concat_axis=0, axis_index_groups=teams, tiled=True)


def tp_moves():
    place = [(y, x, c) for y in range(4) for x in range(2) for c in range(2)]

    def index(y, x, c):
        return ((y % 4) * 2 + x) * 2 + c

    def step(d):
        return [(index(y, x, c), index(y + d, x, c)) for y, x, c in place]

    side = [(index(y, x, c), index(y, 1 - x, c)) for y, x, c in place]
    core = [(index(y, x, c), index(y, x, 1 - c)) for y, x, c in place]
    return step, side, core


def gather_tp(x):
    step, side, core = tp_moves()
    across = lax.ppermute(x, "tp", side)
    near = []
    for d in SHIFTS[1:]:
        near.append(lax.ppermute(x, "tp", step(d)))
    far = [lax.ppermute(b, "tp", side) for b in near[:2]] + [lax.ppermute(across, "tp", step(2))]
    held = [x] + near + [across] + far
    return held + [lax.ppermute(b, "tp", core) for b in held]


def ctx_moves():
    place = [(z, h) for z in range(8) for h in range(2)]
    side = [(z * 2 + h, z * 2 + 1 - h) for z, h in place]
    down = [(z * 2 + h, ((z - 1) % 8) * 2 + h) for z, h in place]
    cross = [(z * 2 + h, ((z + 1) % 8) * 2 + 1 - h) for z, h in place]
    teams = [[(2 * r + odd) * 2 + h for r in range(4)] for odd in range(2) for h in range(2)]
    return (side, down, cross), teams


def local(grad_out, out_weight, gate, key_in, value_in, conv_out, filt, skip_bias):
    channels, toks = gate.shape
    groups = lax.axis_size("ctx")
    per = channels // groups
    blocks = gather_tp(grad_out)
    near, _ = ctx_moves()
    gate_grad, msg, own_block, gated = gated_grads(
        out_weight, gate, conv_out, key_in, value_in, filt, blocks, groups
    )
    whole = swap(msg, "ctx")
    *messages, mine = pack(gated, [own_block] + blocks[1:])
    received = []
    for message, move in zip(messages, near):
        received.append(lax.ppermute(message, "ctx", move))
    core = tp_moves()[2]
    swapped = []
    for r in received:
        swapped.append(lax.ppermute(r, "tp", core))
    result = spectral(whole, dft_tables(groups, per, toks))
    back = swap(result, "ctx")
    own, *parts = weight_parts(mine, received, swapped, result)
    parts = [
        lax.ppermute(part, "ctx", [(z * 2 + h, ((z + 2 * d) % 8) * 2 + h) for z in range(8) for h in range(2)])
        for part, d in zip(parts, (2, 1, 3))
    ]
    filter_grad, key_grad, value_grad, bias_grad = final(back, msg, key_in, value_in, skip_bias)
    weight_grad = sum_parts(own, parts, filter_grad)
    return (gate_grad, key_grad, value_grad, filter_grad, weight_grad, bias_grad.reshape(channels))


def solution(mesh):
    tok = P("tp", "ctx")
    return jax.shard_map(
        local,
        mesh=mesh,
        in_specs=(tok, P("tp", None), tok, tok, tok, tok, tok, P("tp")),
        out_specs=(tok, tok, tok, tok, tok, P("tp")),
        check_vma=False,
    )
```

```python
import functools

import jax
import jax.numpy as jnp
import numpy as np
from jax import lax
from jax.experimental import pallas as pl
from jax.experimental.pallas import tpu as pltpu
from jax.sharding import PartitionSpec as P


bf16 = jnp.bfloat16
f32 = jnp.float32
VM = pl.BlockSpec(memory_space=pltpu.VMEM)
HBM = pl.BlockSpec(memory_space=pltpu.HBM)


def narrow(table):
    return jnp.asarray(table.astype(np.float32).astype(bf16))


def dft_tables(blocks, per, width):
    full = 2 * blocks
    k = np.arange(full)[:, None]
    a = np.arange(blocks)[None, :]
    b = np.arange(width)
    outer = np.exp(-2j * np.pi * ((k * a) % full) / full)
    twist = np.exp(-2j * np.pi * ((k * b[None, :]) % (full * width)) / (full * width))
    inner = np.exp(-2j * np.pi * ((b[:, None] * b[None, :]) % width) / width)
    fwd = narrow(np.repeat(np.stack([outer.real, outer.imag]), per, axis=2))
    back = narrow(np.repeat(np.stack([outer.real.T, outer.imag.T]), per, axis=2))
    inner = narrow(np.concatenate([inner.real, inner.imag], 1))
    return fwd, back, inner, jnp.asarray(np.stack([twist.real, twist.imag]).astype(np.float32))


def dot(left, right):
    return jnp.dot(left, right, preferred_element_type=f32)


def spread_rows(table, per):
    n, lanes = table.shape
    wide = jnp.broadcast_to(table.astype(f32)[:, None, :], (n, per, lanes))
    row = lax.broadcasted_iota(jnp.int32, (n, per, lanes), 1)
    lane = lax.broadcasted_iota(jnp.int32, (n, per, lanes), 2) % per
    return jnp.where(row == lane, wide, 0.0).reshape(n * per, lanes).astype(bf16)


def twisted(re, im, tw_ref, per, sign):
    n, width = tw_ref.shape[1:]
    re = re.reshape(n, per, width)
    im = im.reshape(n, per, width)
    tre = tw_ref[0][:, None, :]
    tim = tw_ref[1][:, None, :] * sign
    return (re * tre - im * tim).reshape(n * per, width), (re * tim + im * tre).reshape(n * per, width)


def inner_dft(re, im, table, sign):
    width = table.shape[0]
    r = dot(re.astype(bf16), table)
    i = dot(im.astype(bf16), table)
    if sign > 0:
        return r[:, :width] - i[:, width:], r[:, width:] + i[:, :width]
    return r[:, :width] + i[:, width:], i[:, :width] - r[:, width:]


def row_scale(x, per):
    wide = x.astype(f32).reshape(-1, per, x.shape[1])
    top = jnp.max(jnp.max(jnp.abs(wide), axis=0), axis=1, keepdims=True)
    top = jnp.where(top > 0.0, top, 1.0)
    wide = wide * (1.0 / top)[None]
    square = jnp.sum(jnp.sum(wide * wide, axis=0), axis=1, keepdims=True)
    root = top * jnp.sqrt(square * (1.0 / (wide.shape[0] * wide.shape[2])))
    return jnp.where(root > 0.0, root, 1.0)[None]


def scaled(x, factor):
    per = factor.shape[1]
    return (x.reshape(-1, per, x.shape[1]) * factor).reshape(x.shape)


def spectral_kernel(msg_ref, *refs, per, blocks, width):
    sources, out_ref, (fwd_ref, back_ref, b_ref, tw_ref), sems = refs[:4], refs[4], refs[5:9], refs[9]
    copies = [pltpu.make_async_copy(src, dst, sems.at[n]) for n, (src, dst) in enumerate(zip(sources, refs[5:9]))]
    for n in (0, 3, 2, 1):
        copies[n].start()
    rows = 2 * blocks * per
    half = blocks * per
    g, p, f = [msg_ref[:, n * per : (n + 1) * per, :].reshape(half, width) for n in range(3)]
    p_top = row_scale(p, per)
    f_top = row_scale(f, per)
    copies[0].wait()
    outer = jnp.concatenate([spread_rows(fwd_ref[c], per) for c in range(2)], 0)
    g1, p1, f1 = [dot(outer, x) for x in (g, p, f)]
    p1 = scaled(p1, 1.0 / p_top)
    f1 = scaled(f1, 1.0 / f_top)
    copies[3].wait()
    copies[2].wait()
    table = b_ref[...]
    gre, gim = inner_dft(*twisted(g1[:rows], g1[rows:], tw_ref, per, 1.0), table, 1)
    zre, zim = inner_dft(*twisted(p1[:rows] + f1[rows:], p1[rows:] - f1[:rows], tw_ref, per, 1.0), table, 1)
    re, im = inner_dft(gre * zre + gim * zim, gim * zre - gre * zim, table, -1)
    re, im = twisted(re, im, tw_ref, per, -1.0)
    scale = 1.0 / (2 * blocks * width)
    re = (re * scale).astype(bf16)
    im = (im * scale).astype(bf16)
    copies[1].wait()
    mat_re, mat_im = [spread_rows(back_ref[c], per) for c in range(2)]
    lag = scaled(dot(mat_re, re) + dot(mat_im, im), p_top)
    conv = scaled(dot(mat_re, im) - dot(mat_im, re), f_top)
    cut = width // 2
    for n, x in enumerate((lag, conv)):
        for side in range(2):
            rows_at = (2 * n + side) * per
            piece = x[:, side * cut : (side + 1) * cut].astype(bf16).reshape(blocks, per, cut)
            out_ref[:, rows_at : rows_at + per, :] = piece
    prod = (g.astype(f32) * p.astype(f32)).reshape(blocks, per, width)
    total = jnp.sum(jnp.sum(prod, axis=0), axis=1, keepdims=True)
    row = lax.broadcasted_iota(jnp.int32, (per, cut), 0)
    lane = lax.broadcasted_iota(jnp.int32, (per, cut), 1) % per
    total = jnp.sum(jnp.where(row == lane, total, 0.0), axis=0, keepdims=True)
    high = total.astype(bf16).astype(f32)
    eighth = per // 2
    which = lax.broadcasted_iota(jnp.int32, (eighth, cut), 0)
    extra = jnp.where(which == 0, high, jnp.where(which == 1, total - high, 0.0)).astype(bf16)
    out_ref[:, 4 * per :, :] = jnp.broadcast_to(extra[None], (blocks, eighth, cut))


def in_hbm(x):
    return pltpu.with_memory_space_constraint(x, pltpu.HBM)


def limit(mib):
    return pltpu.CompilerParams(vmem_limit_bytes=mib << 20)


def cost(flops, bytes_accessed):
    return pl.CostEstimate(flops=flops, bytes_accessed=bytes_accessed, transcendentals=0)


def spectral(msg, tables):
    blocks, triple, width = msg.shape
    per = triple // 3
    return pl.pallas_call(
        functools.partial(spectral_kernel, per=per, blocks=blocks, width=width),
        out_shape=jax.ShapeDtypeStruct((blocks, 4 * per + per // 2, width // 2), bf16),
        in_specs=[VM] + [HBM] * 4,
        out_specs=VM,
        scratch_shapes=[pltpu.VMEM(t.shape, t.dtype) for t in tables] + [pltpu.SemaphoreType.DMA((4,))],
        name="spectral",
        compiler_params=limit(20),
        cost_estimate=cost(2 * 14000 * 256 * 256, 2 << 20),
    )(msg, *[in_hbm(t) for t in tables])


SHIFTS = (0, 1, -1, 2)


def position():
    ctx = lax.axis_index("ctx")
    tp = lax.axis_index("tp")
    return ctx >> 1, ctx & 1, tp >> 2, (tp >> 1) & 1, tp & 1


def gated_kernel(*refs, per):
    sources = refs[:7]
    blocks = list(refs[7:22])
    gate_grad_ref, msg_ref, own_out_ref, gated_ref = refs[22:26]
    buffers, sems = refs[26:33], refs[33]
    copies = [pltpu.make_async_copy(src, dst, sems.at[n]) for n, (src, dst) in enumerate(zip(sources, buffers))]
    for n in (1, 0, 2, 3, 4, 5, 6):
        copies[n].start()
    own_ref, w_ref, gate_ref, conv_ref, key_ref, value_ref, filt_ref = buffers
    groups, _, width = msg_ref.shape
    _, _, y, xl, core = position()
    for n in (0, 2, 3, 4, 5, 6):
        copies[n].wait()
    own_out_ref[...] = own_ref[...]
    gated_ref[...] = (gate_ref[...].astype(f32) * conv_ref[...].astype(f32)).astype(bf16)
    product = (key_ref[...].astype(f32) * value_ref[...].astype(f32)).astype(bf16)
    msg_ref[:, per : 2 * per, :] = product.reshape(groups, per, width)
    msg_ref[:, 2 * per :, :] = filt_ref[...].reshape(groups, per, width)
    copies[1].wait()
    total = jnp.zeros(gate_grad_ref.shape, f32)
    for n, block in enumerate([own_ref] + blocks):
        index = (((y - SHIFTS[n % 4]) & 3) * 2 + (xl ^ (n // 4 % 2))) * 2 + (core ^ (n // 8))
        total = total + dot(w_ref[:, pl.ds(pl.multiple_of(index * width, width), width)], block[...])
    gate_grad_ref[...] = (total * conv_ref[...].astype(f32)).astype(bf16)
    msg_ref[:, :per, :] = (total * gate_ref[...].astype(f32)).astype(bf16).reshape(groups, per, width)


def gated_grads(weight, gate, conv_out, key_in, value_in, filt, blocks, groups):
    channels, width = gate.shape
    per = channels // groups
    small = pltpu.VMEM(gate.shape, bf16)
    shape = jax.ShapeDtypeStruct(gate.shape, bf16)
    held = [blocks[0], weight, gate, conv_out, key_in, value_in, filt]
    return pl.pallas_call(
        functools.partial(gated_kernel, per=per),
        out_shape=(shape, jax.ShapeDtypeStruct((groups, 3 * per, width), bf16), shape, shape),
        in_specs=[HBM] * 7 + [VM] * 15,
        out_specs=(VM,) * 4,
        scratch_shapes=[small, pltpu.VMEM(weight.shape, bf16)] + [small] * 5 + [pltpu.SemaphoreType.DMA((7,))],
        name="gated_grads",
        compiler_params=limit(6),
        cost_estimate=cost(2 * gate.size * weight.shape[1], 5 << 20),
    )(*[in_hbm(x) for x in held], *blocks[1:])


def pack_kernel(gated_ref, *refs):
    blocks = refs[:16]
    side_ref, down_ref, cross_ref, mine_ref = refs[16:]
    z, h, y, xl, core = position()
    for ref in (side_ref, down_ref, cross_ref):
        ref[2] = gated_ref[...]
    mine_ref[4] = gated_ref[...]
    keep = (core ^ h) * 2 + (xl ^ (z & 1))
    for q in range(4):

        @pl.when(keep == q)
        def _():
            for n, d in enumerate(SHIFTS):
                row = (y - d) & 3
                mine_ref[row] = blocks[q * 4 + n][...]

                @pl.when((row >> 1) == core)
                def _():
                    for ref, turn in ((side_ref, 2), (down_ref, 1), (cross_ref, 3)):
                        ref[row & 1] = blocks[(q ^ turn) * 4 + n][...]


def pack(gated, blocks):
    shape = gated.shape
    return pl.pallas_call(
        pack_kernel,
        out_shape=tuple(jax.ShapeDtypeStruct((n,) + shape, bf16) for n in (3, 3, 3, 5)),
        in_specs=[VM] * 17,
        out_specs=(VM,) * 4,
        name="pack",
        compiler_params=limit(3),
        cost_estimate=cost(gated.size, 4 << 20),
    )(gated, *blocks)


def join_kernel(after_hbm, *refs):
    out_ref = refs[3]
    for m in range(3):
        out_ref[2 * m : 2 * m + 2] = refs[m][:2]


def join(received, after):
    shape = received[0].shape[1:]
    return pl.pallas_call(
        join_kernel,
        out_shape=jax.ShapeDtypeStruct((6,) + shape, bf16),
        in_specs=[HBM] + [VM] * 3,
        out_specs=VM,
        name="join",
        compiler_params=limit(3),
        cost_estimate=cost(256 * 256, 2 << 20),
    )(in_hbm(after), *received)


def weight_kernel(after_hbm, mine_ref, *refs):
    received = refs[:3]
    swapped = [refs[3].at[pl.ds(2 * m, 2)] for m in range(3)]
    own_ref, *outs, sum_ref = refs[4:]
    z, _, _, _, core = position()

    def outer(rows, block):
        return lax.dot_general(rows, block, (((1,), (1,)), ((), ())), preferred_element_type=f32)

    rows = [mine_ref[4]] + [ref[2] for ref in received]
    for half, source in ((core, received), (1 - core, swapped)):
        for i in range(2):
            r = 2 * half + i
            total = outer(rows[0], mine_ref[r])
            for m in range(3):
                total = total + outer(rows[m + 1], source[m][i])
            sum_ref[r] = total
    own_ref[...] = sum_ref[z >> 1]
    for out, d in zip(outs, (2, 1, 3)):
        out[...] = sum_ref[((z >> 1) + d) & 3].astype(bf16)


def weight_parts(mine, received, swapped, after):
    shape = mine.shape[1:]
    return pl.pallas_call(
        weight_kernel,
        out_shape=(jax.ShapeDtypeStruct(shape, f32),) + (jax.ShapeDtypeStruct(shape, bf16),) * 3,
        in_specs=[HBM] + [VM] * 5,
        out_specs=(VM,) * 4,
        scratch_shapes=[pltpu.VMEM((4,) + shape, f32)],
        name="weight_parts",
        compiler_params=limit(8),
        cost_estimate=cost(2 * 16 * 256**3, 4 << 20),
    )(in_hbm(after), mine, *received, swapped)


def final_kernel(back_ref, msg_ref, key_ref, value_ref, skip_ref, filter_ref, dkey_ref, dvalue_ref, bias_ref, *, per):
    groups, _, cut = back_ref.shape
    channels = groups * per

    def whole(n):
        pieces = [back_ref[:, (2 * n + side) * per : (2 * n + side + 1) * per, :] for side in range(2)]
        return jnp.concatenate([piece.reshape(channels, cut) for piece in pieces], 1)

    filter_ref[...] = whole(0)
    conv = whole(1).astype(f32)
    grad = msg_ref[:, :per, :].reshape(channels, 2 * cut).astype(f32)
    total = (conv + skip_ref[...] * grad).astype(bf16).astype(f32)
    dkey_ref[...] = (total * value_ref[...].astype(f32)).astype(bf16)
    dvalue_ref[...] = (total * key_ref[...].astype(f32)).astype(bf16)
    extra = back_ref[:, 4 * per :, :].astype(f32)
    pair = extra[:, 0, :] + extra[:, 1, :]
    pair = jnp.concatenate([pair] * (channels // cut), 1)
    row = lax.broadcasted_iota(jnp.int32, (groups, channels), 0)
    lane = lax.broadcasted_iota(jnp.int32, (groups, channels), 1) // per
    bias_ref[...] = jnp.sum(jnp.where(row == lane, pair, 0.0), axis=0, keepdims=True)


def final(back, msg, key_in, value_in, skip_bias):
    shape = jax.ShapeDtypeStruct(key_in.shape, bf16)
    channels = key_in.shape[0]
    per = channels // back.shape[0]
    return pl.pallas_call(
        functools.partial(final_kernel, per=per),
        out_shape=(shape, shape, shape, jax.ShapeDtypeStruct((1, channels), f32)),
        in_specs=[VM] * 5,
        out_specs=(VM,) * 4,
        name="final",
        compiler_params=limit(6),
        cost_estimate=cost(8 * key_in.size, 1 << 20),
    )(back, msg, key_in, value_in, skip_bias[:, None])


def sum_kernel(after_hbm, own_ref, one_ref, two_ref, three_ref, out_ref):
    total = own_ref[...] + one_ref[...].astype(f32)
    out_ref[...] = total + (two_ref[...].astype(f32) + three_ref[...].astype(f32))


def sum_parts(own, parts, after):
    return pl.pallas_call(
        sum_kernel,
        out_shape=jax.ShapeDtypeStruct(own.shape, f32),
        in_specs=[HBM] + [VM] * 4,
        out_specs=VM,
        name="sum_parts",
        compiler_params=limit(3),
        cost_estimate=cost(4 * own.size, 1 << 20),
    )(in_hbm(after), own, *parts)


def swap(x, axis, teams=None):
    return lax.all_to_all(x, axis, split_axis=0, concat_axis=0, axis_index_groups=teams, tiled=True)


def tp_moves():
    place = [(y, x, c) for y in range(4) for x in range(2) for c in range(2)]

    def index(y, x, c):
        return ((y % 4) * 2 + x) * 2 + c

    def step(d):
        return [(index(y, x, c), index(y + d, x, c)) for y, x, c in place]

    side = [(index(y, x, c), index(y, 1 - x, c)) for y, x, c in place]
    core = [(index(y, x, c), index(y, x, 1 - c)) for y, x, c in place]
    return step, side, core


def gather_tp(x):
    step, side, core = tp_moves()
    across = lax.ppermute(x, "tp", side)
    near = []
    for d in SHIFTS[1:]:
        near.append(lax.ppermute(x, "tp", step(d)))
    far = [lax.ppermute(b, "tp", side) for b in near[:2]] + [lax.ppermute(across, "tp", step(2))]
    held = [x] + near + [across] + far
    return held + [lax.ppermute(b, "tp", core) for b in held]


def ctx_moves():
    place = [(z, h) for z in range(8) for h in range(2)]
    side = [(z * 2 + h, z * 2 + 1 - h) for z, h in place]
    down = [(z * 2 + h, ((z - 1) % 8) * 2 + h) for z, h in place]
    cross = [(z * 2 + h, ((z + 1) % 8) * 2 + 1 - h) for z, h in place]
    teams = [[(2 * r + odd) * 2 + h for r in range(4)] for odd in range(2) for h in range(2)]
    return (side, down, cross), teams


def local(grad_out, out_weight, gate, key_in, value_in, conv_out, filt, skip_bias):
    channels, toks = gate.shape
    groups = lax.axis_size("ctx")
    per = channels // groups
    blocks = gather_tp(grad_out)
    near, _ = ctx_moves()
    gate_grad, msg, own_block, gated = gated_grads(
        out_weight, gate, conv_out, key_in, value_in, filt, blocks, groups
    )
    whole = swap(msg, "ctx")
    *messages, mine = pack(gated, [own_block] + blocks[1:])
    received = []
    for message, move in zip(messages, near):
        received.append(lax.ppermute(message, "ctx", move))
    core = tp_moves()[2]
    result = spectral(whole, dft_tables(groups, per, toks))
    swapped = lax.ppermute(join(received, result), "tp", core)
    back = swap(result, "ctx")
    own, *parts = weight_parts(mine, received, swapped, result)
    parts = [
        lax.ppermute(part, "ctx", [(z * 2 + h, ((z + 2 * d) % 8) * 2 + h) for z in range(8) for h in range(2)])
        for part, d in zip(parts, (2, 1, 3))
    ]
    filter_grad, key_grad, value_grad, bias_grad = final(back, msg, key_in, value_in, skip_bias)
    weight_grad = sum_parts(own, parts, filter_grad)
    return (gate_grad, key_grad, value_grad, filter_grad, weight_grad, bias_grad.reshape(channels))


def solution(mesh):
    tok = P("tp", "ctx")
    return jax.shard_map(
        local,
        mesh=mesh,
        in_specs=(tok, P("tp", None), tok, tok, tok, tok, tok, P("tp")),
        out_specs=(tok, tok, tok, tok, tok, P("tp")),
        check_vma=False,
    )
```
